512 devices in a mesh: gx: 64 (over z_lo, x, core), yz: 8 (over y, z_hi).
Axes of the slice: x: 4, y: 4, z: 16 (z_hi: 2, z_lo: 8; z = z_hi * 8 + z_lo), core: 2. Of those that a mesh axis runs over, the one named last changes fastest.
Arguments:
- solution: float32 [4, 512, 64, 3, 128], P(None, 'gx', 'yz'), may hold values from -6 to 6
- residual: float32 [4, 512, 64, 3, 128], P(None, 'gx', 'yz'), may hold values from -6 to 6
- direction: float32 [4, 512, 64, 3, 128], P(None, 'gx', 'yz'), may hold values from -6 to 6
- stiffness: float32 [512, 64, 128], P('gx', 'yz'), may hold values from 0.5 to 13.52
- coupling: float32 [512, 64, 128], P('gx', 'yz'), may hold values from 0.5 to 2
- lower_factor: float32 [64, 8, 384, 384], P('gx', 'yz'), may hold values from -0.122474487 to 1
- upper_factor: float32 [64, 8, 384, 384], P('gx', 'yz'), may hold values from -0.122474487 to 2, as said below
- pivot_order: int32 [64, 8, 384], P('gx', 'yz'), may hold values from 0 to 383, each once within a row
- coarse_basis: float32 [4, 512, 64, 128], P(None, 'gx', 'yz'), may hold values from 0.2 to 1
- coarse_inverse: float32 [64, 8, 12, 6144], P('gx', 'yz'), may hold values from -0.00024917498 to 0.009765625
- inner_prior: float32 [4], replicated, may hold values from 6291456 to 25165824
Outputs:
- solution_next: float32 [4, 512, 64, 3, 128], P(None, 'gx', 'yz')
- residual_next: float32 [4, 512, 64, 3, 128], P(None, 'gx', 'yz')
- direction_next: float32 [4, 512, 64, 3, 128], P(None, 'gx', 'yz')
- inner_next: float32 [4], replicated
The draws below stay inside these ranges and needn't reach their ends.
Inputs may be any that keep to these rules, and one draw needn't show every extreme that they name: `upper_factor`: upper triangular with positive diagonal.
All inputs are finite; a program needn't handle non-finite values.
Results may differ from the reference program's by a relative error of at most 0.000067.
Values sent between devices are 32-bit elements; how exact they have to be, the bound alone decides.
No kernel may reach another device: no remote copies, remote signals or barrier semaphores. Data moves between devices by JAX's collectives and lax.ppermute only.
A program may use at most 64 MiB of HBM per device.

```python
import math
import jax
import jax.numpy as jnp
from jax import lax

CASES = 4
COMP = 3
NX = 8
NY = 8
NZ = 128
NP = 4
LINE = 384
PRIMAL = 12
GX = 512
GY = 64
NCOARSE = 6144
N_GX = 64
N_YZ = 8


def draw_stiffness(key, part):
    seeded = jax.random.fold_in(key, 101)
    field_shape = (GX, GY, NZ)
    rows_ramp = jnp.arange(GX, dtype=jnp.float32) / max(GX - 1, 1)
    cols_ramp = jnp.arange(GY, dtype=jnp.float32) / max(GY - 1, 1)
    base = jnp.exp(jax.random.uniform(seeded, field_shape, jnp.float32, jnp.log(0.5), jnp.log(2.0)))
    slope = 0.8
    ramp = (1.0 + slope * rows_ramp)[:, None, None] * (1.0 + slope * cols_ramp)[None, :, None]
    return base * ramp


def triangle_noise(seeded):
    field_shape = (N_GX, N_YZ, LINE, LINE)
    noise = 0.6 * jax.random.truncated_normal(seeded, -4.0, 4.0, field_shape, jnp.float32)
    return noise / LINE ** 0.5


def draw_lower_factor(key, part):
    noise = triangle_noise(jax.random.fold_in(key, 202))
    rows_index = jnp.arange(LINE)[:, None]
    cols_index = jnp.arange(LINE)[None, :]
    return jnp.where(rows_index > cols_index, noise, 0.0) + jnp.where(rows_index == cols_index, 1.0, 0.0)


def draw_upper_factor(key, part):
    noise = triangle_noise(jax.random.fold_in(key, 303))
    diagonal = jnp.exp(jax.random.uniform(jax.random.fold_in(key, 404), (N_GX, N_YZ, LINE, 1), jnp.float32, jnp.log(0.5), jnp.log(2.0)))
    rows_index = jnp.arange(LINE)[:, None]
    cols_index = jnp.arange(LINE)[None, :]
    return jnp.where(rows_index < cols_index, noise, 0.0) + jnp.where(rows_index == cols_index, diagonal, 0.0)


def draw_coarse_inverse(key, part):
    seeded = jax.random.fold_in(key, 505)
    field_shape = (N_GX, N_YZ, PRIMAL, NCOARSE)
    noise = jax.random.truncated_normal(seeded, -4.0, 4.0, field_shape, jnp.float32)
    noise = noise / NCOARSE ** 0.5
    device_index = jnp.arange(N_GX)[:, None] * N_YZ + jnp.arange(N_YZ)[None, :]
    own_column = device_index[:, :, None, None] * PRIMAL + jnp.arange(PRIMAL)[None, None, :, None]
    columns = jnp.arange(NCOARSE)[None, None, None, :]
    return (noise + jnp.where(own_column == columns, 1.0, 0.0)) * (40.0 / (NX * NY * NZ))


def block_levels(key, shape, cuts, smallest, top_value):
    def one(axis_at, shards_of):
        draws = jax.random.uniform(jax.random.fold_in(jax.random.fold_in(key, 6), axis_at), (shards_of,), jnp.float32, smallest / len(cuts), top_value / len(cuts))
        return jnp.repeat(jnp.exp(draws), shape[axis_at] // shards_of).reshape((-1,) + (1,) * (len(shape) - axis_at - 1))

    gain = one(*cuts[0])
    for cut in cuts[1:]:
        gain = gain * one(*cut)
    return gain


def scatter_about(stream_key, extent, scale, limit, split=(), held_as=jnp.bfloat16):
    values = scale * jax.random.normal(stream_key, extent, jnp.float32)
    if split:
        values = values * block_levels(stream_key, extent, split, -0.22, 0.18)
    return jnp.clip(values, -limit, limit).astype(held_as)


def setup_inputs(seed: int = 0) -> dict:
    splits = jax.random.split(jax.random.key(seed), 12)
    return {
        "solution": scatter_about(splits[0], (CASES, GX, GY, COMP, NZ), 1.0, 6.0, ((1, 64), (2, 8)), jnp.float32),
        "residual": scatter_about(splits[1], (CASES, GX, GY, COMP, NZ), 1.0, 6.0, ((1, 64), (2, 8)), jnp.float32),
        "direction": scatter_about(splits[2], (CASES, GX, GY, COMP, NZ), 1.0, 6.0, ((1, 64), (2, 8)), jnp.float32),
        "stiffness": draw_stiffness(jax.random.fold_in(splits[11], 71), 0),
        "coupling": jnp.clip(jnp.exp(math.log(2.0) - 1.3862944 * jax.random.uniform(splits[4], (GX, GY, NZ), jnp.float32) ** block_levels(splits[4], (GX, GY, NZ), ((0, 64), (1, 8)), -0.2, 0.2)), 0.5, 2.0),
        "lower_factor": draw_lower_factor(jax.random.fold_in(splits[11], 71), 0),
        "upper_factor": draw_upper_factor(jax.random.fold_in(splits[11], 71), 0),
        "pivot_order": jax.vmap(lambda own: jax.random.permutation(own, LINE))(jax.random.split(splits[7], N_GX * N_YZ)).reshape((N_GX, N_YZ, LINE)).astype(jnp.int32),
        "coarse_basis": jnp.clip(0.2 + 0.8 * jax.random.uniform(splits[8], (NP, GX, GY, NZ), jnp.float32) ** block_levels(splits[8], (NP, GX, GY, NZ), ((1, 64), (2, 8)), -0.2, 0.2), 0.2, 1.0),
        "coarse_inverse": draw_coarse_inverse(jax.random.fold_in(splits[11], 71), 0),
        "inner_prior": jnp.clip(jax.random.uniform(splits[10], (CASES,), jnp.float32, 6291456, 25165824), 6291456, 25165824),
    }


precise = lax.Precision.HIGHEST


def operate(direction, stiffness, coupling):
    scaled = stiffness[None, :, :, None, :] * direction
    padded = jnp.pad(scaled, ((0, 0), (1, 1), (1, 1), (0, 0), (1, 1)))
    beside = padded[:, 2:, 1:-1, :, 1:-1] + padded[:, :-2, 1:-1, :, 1:-1]
    beside = beside + padded[:, 1:-1, 2:, :, 1:-1] + padded[:, 1:-1, :-2, :, 1:-1]
    beside = beside + padded[:, 1:-1, 1:-1, :, 2:] + padded[:, 1:-1, 1:-1, :, :-2]
    return stiffness[None, :, :, None, :] * (6.0 * scaled - beside) + coupling[None, :, :, None, :] * jnp.sum(direction, axis=3, keepdims=True)


def solve_lines(field, lower_factor, upper_factor, pivot_order):
    blocks = field.reshape(CASES, N_GX, NX, N_YZ, NY, LINE)
    pivots = jnp.broadcast_to(pivot_order[None, :, None, :, None, :], blocks.shape)
    permuted = jnp.take_along_axis(blocks, pivots, axis=5)
    middle = jnp.einsum("gyij,cgaybj->cgaybi", lower_factor, permuted, precision=precise)
    solved = jnp.einsum("gyij,cgaybj->cgaybi", upper_factor, middle, precision=precise)
    inverse_order = jnp.argsort(pivot_order, axis=-1).astype(jnp.int32)
    restore = jnp.broadcast_to(inverse_order[None, :, None, :, None, :], blocks.shape)
    return jnp.take_along_axis(solved, restore, axis=5).reshape(field.shape)


def across(field):
    zero_rows = jnp.zeros_like(field[:, :1])
    from_left = jnp.concatenate([zero_rows, field[:, :-1]], axis=1)
    from_right = jnp.concatenate([field[:, 1:], zero_rows], axis=1)
    zero_cols = jnp.zeros_like(field[:, :, :1])
    from_below = jnp.concatenate([zero_cols, field[:, :, :-1]], axis=2)
    from_above = jnp.concatenate([field[:, :, 1:], zero_cols], axis=2)
    global_rows = jnp.arange(field.shape[1])
    global_cols = jnp.arange(field.shape[2])
    first_rows = (global_rows % NX == 0)[None, :, None, None, None]
    last_rows = (global_rows % NX == NX - 1)[None, :, None, None, None]
    first_cols = (global_cols % NY == 0)[None, None, :, None, None]
    last_cols = (global_cols % NY == NY - 1)[None, None, :, None, None]
    neighbours = jnp.where(first_rows, from_left, 0.0) + jnp.where(last_rows, from_right, 0.0)
    neighbours = neighbours + jnp.where(first_cols, from_below, 0.0) + jnp.where(last_cols, from_above, 0.0)
    return field + 0.5 * neighbours


def reference(solution, residual, direction, stiffness, coupling, lower_factor, upper_factor, pivot_order, coarse_basis, coarse_inverse, inner_prior):
    applied = operate(direction, stiffness, coupling)
    curvature = jnp.sum(direction * applied, axis=(1, 2, 3, 4))
    step_size = inner_prior / curvature
    step_field = step_size[:, None, None, None, None]
    solution_next = solution + step_field * direction
    residual_next = residual - step_field * applied
    smoothed = across(solve_lines(residual_next, lower_factor, upper_factor, pivot_order))
    basis_blocks = coarse_basis.reshape(NP, N_GX, NX, N_YZ, NY, NZ)
    field_blocks = residual_next.reshape(CASES, N_GX, NX, N_YZ, NY, COMP, NZ)
    primal = jnp.einsum("pgaybz,cgaybkz->cgykp", basis_blocks, field_blocks, precision=precise).reshape(CASES, NCOARSE)
    coarse_values = jnp.einsum("gyjm,cm->cgyj", coarse_inverse, primal, precision=precise)
    coarse_values = coarse_values.reshape(CASES, N_GX, N_YZ, COMP, NP)
    correction = jnp.einsum("pgaybz,cgykp->cgaybkz", basis_blocks, coarse_values, precision=precise)
    preconditioned = smoothed + correction.reshape(residual.shape)
    inner_next = jnp.sum(residual_next * preconditioned, axis=(1, 2, 3, 4))
    growth = (inner_next / inner_prior)[:, None, None, None, None]
    direction_next = preconditioned + growth * direction
    return solution_next, residual_next, direction_next, inner_next
```

```python
import jax
import jax.numpy as jnp
from jax import lax
from jax.sharding import Mesh, PartitionSpec as P

precise = lax.Precision.HIGHEST

DEPTH = ("zl", "zh")
PLANE = ("x", "c", "y")
GX_AXES = ("zl", "x", "c")
YZ_AXES = ("y", "zh")
SIZES = {"zl": 8, "x": 4, "c": 2, "y": 4, "zh": 2}
N_DEPTH = 16
N_PLANE = 32


def exchange(block, axes, count):
    spread = jnp.broadcast_to(block[None], (count,) + block.shape)
    return lax.all_to_all(spread, axes, 0, 0, tiled=True)


def gather_rows(row):
    line = exchange(row, DEPTH, N_DEPTH).reshape(N_DEPTH, 128)
    return exchange(line, PLANE, N_PLANE).reshape(N_PLANE * N_DEPTH, 128)


def total_rows(row):
    line = exchange(row, DEPTH, N_DEPTH)
    part = jnp.sum(line, axis=0)
    return jnp.sum(exchange(part, PLANE, N_PLANE), axis=0)


def faces(field):
    found = []
    for axes, dim in ((YZ_AXES, 2), (GX_AXES, 1)):
        count = 1
        for name in axes:
            count *= SIZES[name]
        up = [(i, i + 1) for i in range(count - 1)]
        down = [(i + 1, i) for i in range(count - 1)]
        last = field.shape[dim]
        head = lax.slice_in_dim(field, 0, 1, axis=dim)
        tail = lax.slice_in_dim(field, last - 1, last, axis=dim)
        found.append((lax.ppermute(tail, axes, up), lax.ppermute(head, axes, down)))
    return found[1] + found[0]


def beside(field, below, above, dim):
    size = field.shape[dim]
    lower = jnp.concatenate([below, lax.slice_in_dim(field, 0, size - 1, axis=dim)], axis=dim)
    upper = jnp.concatenate([lax.slice_in_dim(field, 1, size, axis=dim), above], axis=dim)
    return lower + upper


def edges(field, below, above, dim):
    shape = list(field.shape)
    shape[dim] -= 2
    return jnp.concatenate([below, jnp.zeros(shape, field.dtype), above], axis=dim)


def per_device(
    solution,
    residual,
    direction,
    stiffness,
    coupling,
    lower_factor,
    upper_factor,
    pivot_order,
    coarse_basis,
    coarse_inverse,
    inner_prior,
):
    cases = residual.shape[0]
    stiff = stiffness[None, :, :, None, :]
    scaled = stiff * direction
    halo = faces(scaled)

    pivots = pivot_order.reshape(-1)
    width = pivots.shape[0]
    chosen = (pivots[:, None] == jnp.arange(width)[None, :]).astype(jnp.float32)
    product = jnp.dot(upper_factor[0, 0], lower_factor[0, 0], precision=precise)
    inner = jnp.dot(product, chosen, precision=precise)
    operator = lax.dot_general(
        chosen, inner, (((0,), (0,)), ((), ())), precision=precise
    )

    def solve(field):
        rows = field.reshape(-1, width)
        return lax.dot_general(
            rows, operator, (((1,), (1,)), ((), ())), precision=precise
        ).reshape(field.shape)

    def restrict(field):
        return jnp.einsum("pxyz,cxykz->ckp", coarse_basis, field, precision=precise).reshape(-1)

    coarse_rows = (
        coarse_inverse.reshape(12, 8, 4, 2, 4, 2, 12)
        .transpose(2, 3, 4, 1, 5, 6, 0)
        .reshape(512, 144)
    )
    solved_r = solve(residual)
    primal_r = restrict(residual)

    zero = jnp.zeros_like(scaled[..., :1])
    upward = jnp.concatenate([scaled[..., 1:], zero], axis=4)
    downward = jnp.concatenate([zero, scaled[..., :-1]], axis=4)
    around = beside(scaled, halo[0], halo[1], 1) + beside(scaled, halo[2], halo[3], 2)
    applied = stiff * (6.0 * scaled - around - upward - downward) + coupling[
        None, :, :, None, :
    ] * jnp.sum(direction, axis=3, keepdims=True)
    curve_part = jnp.sum(direction * applied, axis=(1, 2, 3, 4))
    solved_w = solve(applied)
    primal_w = restrict(applied)
    outer = faces(jnp.concatenate([solved_r, solved_w], axis=0))

    row = jnp.concatenate([primal_r, primal_w, curve_part, jnp.zeros((28,), jnp.float32)])
    table = gather_rows(row.reshape(1, 128))
    curvature = jnp.sum(table[:, 96:100], axis=0)
    step_size = inner_prior / curvature
    step_field = step_size[:, None, None, None, None]
    step_lanes = jnp.repeat(step_size, 12)

    primal_all = table[:, :48] - step_lanes[None, :] * table[:, 48:96]
    primal_own = (primal_r - step_lanes * primal_w).reshape(cases, 12)
    mixed = lax.dot_general(
        primal_all, coarse_rows, (((0,), (0,)), ((), ())), precision=precise
    ).reshape(cases, 12, 12, 12)
    same = jnp.eye(12, dtype=jnp.float32)[None, :, :, None]
    coarse_values = jnp.sum(mixed * same, axis=(1, 2))

    residual_next = residual - step_field * applied
    solved = solved_r - step_field * solved_w
    near = [face[:cases] - step_field * face[cases:] for face in outer]
    smoothed = solved + 0.5 * (
        edges(solved, near[0], near[1], 1) + edges(solved, near[2], near[3], 2)
    )
    inner_part = jnp.sum(residual_next * smoothed, axis=(1, 2, 3, 4)) + jnp.sum(
        primal_own * coarse_values, axis=1
    )
    inner_row = jnp.concatenate([inner_part, jnp.zeros((124,), jnp.float32)])
    inner_next = total_rows(inner_row.reshape(1, 128))[0, :4]
    growth = (inner_next / inner_prior)[:, None, None, None, None]
    correction = jnp.einsum(
        "pxyz,ckp->cxykz",
        coarse_basis,
        coarse_values.reshape(cases, 3, 4),
        precision=precise,
    )
    direction_next = smoothed + correction + growth * direction
    solution_next = solution + step_field * direction
    return (solution_next, residual_next, direction_next, inner_next)


def solution(mesh):
    fine = Mesh(mesh.devices.reshape(8, 4, 2, 4, 2), ("zl", "x", "c", "y", "zh"))
    field = P(None, GX_AXES, YZ_AXES, None, None)
    block = P(GX_AXES, YZ_AXES, None)
    factor = P(GX_AXES, YZ_AXES, None, None)
    in_specs = (
        field,
        field,
        field,
        block,
        block,
        factor,
        factor,
        block,
        P(None, GX_AXES, YZ_AXES, None),
        factor,
        P(),
    )
    return jax.shard_map(
        per_device,
        mesh=fine,
        in_specs=in_specs,
        out_specs=(field, field, field, P()),
        check_vma=False,
    )
```

```python
import jax
import jax.numpy as jnp
from jax import lax
from jax.experimental import pallas as pl
from jax.experimental.pallas import tpu as pltpu
from jax.sharding import Mesh, PartitionSpec as P


DEPTH = ("zh", "zl")
PLANE = ("x", "c", "y")
GX_AXES = ("zl", "x", "c")
YZ_AXES = ("y", "zh")
N_DEPTH = 16
N_PLANE = 32
N_GX = 64
N_YZ = 8

CASES, NX, COMP, NY, NZ = 4, 8, 3, 8, 128
NP = 4
PRIMAL = COMP * NP
LINE = COMP * NZ
TILES = CASES * NX * COMP
FIELD = (CASES, NX, COMP, NY, NZ)
f32 = jnp.float32
bf16 = jnp.bfloat16
NT = (((1,), (1,)), ((), ()))
NN = (((1,), (0,)), ((), ()))


def mxu(a, b, dims):
    return lax.dot_general(a, b, dims, preferred_element_type=f32)


def halves(a):
    high = a.astype(bf16)
    return high, (a - high.astype(f32)).astype(bf16)


def thirds(a):
    high = a.astype(bf16)
    rest = a - high.astype(f32)
    mid = rest.astype(bf16)
    return high, mid, (rest - mid.astype(f32)).astype(bf16)


def product(a, b, dims):
    a0, a1, a2 = thirds(a)
    b0, b1, b2 = thirds(b)
    small = mxu(a0, b2, dims) + mxu(a2, b0, dims) + mxu(a1, b1, dims)
    return (small + (mxu(a0, b1, dims) + mxu(a1, b0, dims))) + mxu(a0, b0, dims)


def picked(chosen, b, dims):
    b0, b1, b2 = thirds(b)
    return (mxu(chosen, b2, dims) + mxu(chosen, b1, dims)) + mxu(chosen, b0, dims)


def lane_sums(a):
    ones = jnp.ones((a.shape[1], 128), bf16)
    a0, a1, a2 = thirds(a)
    return (mxu(a2, ones, NN) + mxu(a1, ones, NN)) + mxu(a0, ones, NN)


def lane_row(a):
    rows = a.shape[0]
    if rows < 128:
        a = jnp.concatenate([a, jnp.zeros((128 - rows, 128), f32)], axis=0)
    ones = jnp.ones((8, 128), bf16)
    a0, a1, a2 = thirds(a)
    return ((mxu(ones, a2, NT) + mxu(ones, a1, NT)) + mxu(ones, a0, NT))[0:1]


def restricted(basis, field):
    rows = []
    for c in range(CASES):
        for k in range(COMP):
            for p in range(NP):
                total = basis[p, 0] * field[c, 0, k]
                for x in range(1, NX):
                    total = total + basis[p, x] * field[c, x, k]
                rows.append(jnp.sum(total, axis=0, keepdims=True))
    return jnp.concatenate(rows, axis=0)


def local_solve(field, operator_ref, out_ref):
    total = None
    for k in range(COMP):
        rows = field[:, :, k].reshape(CASES * NX * NY, NZ)
        part = product(rows, operator_ref[k * NZ : (k + 1) * NZ, :], NN)
        total = part if total is None else total + part
    for k in range(COMP):
        out_ref[:, :, k] = total[:, k * NZ : (k + 1) * NZ].reshape(CASES, NX, NY, NZ)


def side_rows(ref, out_ref, y, base):
    for c in range(CASES):
        for x in range(NX):
            for k in range(COMP):
                row = base + (c * NX + x) * COMP + k
                out_ref[row : row + 1, :] = ref[c, x, k, y : y + 1, :]


def faces_kernel(direction, stiffness, low_x, high_x, low_y, high_y):
    for x, out in ((0, low_x), (NX - 1, high_x)):
        out[...] = direction[:, x] * stiffness[x][None, None]
    for y, out in ((0, low_y), (NY - 1, high_y)):
        for c in range(CASES):
            for x in range(NX):
                for k in range(COMP):
                    row = (c * NX + x) * COMP + k
                    out[row : row + 1, :] = (
                        direction[c, x, k, y : y + 1, :] * stiffness[x, y : y + 1, :]
                    )


def prepare_kernel(residual, lower, upper, pivots, basis, operator, solved, primal):
    order = pivots[...]
    at = lax.broadcasted_iota(jnp.int32, (LINE, LINE), 0)
    chosen = jnp.where(at == order, 1.0, 0.0).astype(bf16)
    both = product(upper[...], lower[...], NN)
    rows = picked(chosen, both, NN)
    operator[...] = picked(chosen, rows, NT)
    local_solve(residual, operator, solved)
    primal[...] = lane_sums(restricted(basis, residual))


def by_depth_kernel(inverse, by_depth):
    for r in range(PRIMAL):
        for half in range(2):
            for part in range(3):
                at = r * 48 + half * 3 + part
                by_depth[r, half, :, part * 128 : (part + 1) * 128] = inverse[
                    pl.ds(at, 8, stride=6), :
                ]


def applied_kernel(
    direction, stiffness, coupling, below_x, above_x, below_y, above_y,
    basis, operator, solved_r, primal_r,
    applied, solved, primal, row, low_x, high_x, low_y, high_y,
):
    y_at = lax.broadcasted_iota(jnp.int32, (NY, NZ), 0)
    z_at = lax.broadcasted_iota(jnp.int32, (NY, NZ), 1)
    first_y, last_y = y_at == 0, y_at == NY - 1
    first_z, last_z = z_at == 0, z_at == NZ - 1
    curves = []
    for c in range(CASES):
        curve = None
        for x in range(NX):
            stiff = stiffness[x]
            total = direction[c, x, 0] + direction[c, x, 1] + direction[c, x, 2]
            spread = coupling[x] * total
            for k in range(COMP):
                here = direction[c, x, k]
                mine = stiff * here
                left = below_x[c, k] if x == 0 else stiffness[x - 1] * direction[c, x - 1, k]
                right = above_x[c, k] if x == NX - 1 else stiffness[x + 1] * direction[c, x + 1, k]
                at = (c * NX + x) * COMP + k
                down = jnp.where(
                    first_y,
                    jnp.broadcast_to(below_y[at : at + 1, :], (NY, NZ)),
                    pltpu.roll(mine, 1, 0),
                )
                up = jnp.where(
                    last_y,
                    jnp.broadcast_to(above_y[at : at + 1, :], (NY, NZ)),
                    pltpu.roll(mine, NY - 1, 0),
                )
                before = jnp.where(first_z, 0.0, pltpu.roll(mine, 1, 1))
                after = jnp.where(last_z, 0.0, pltpu.roll(mine, NZ - 1, 1))
                around = (left + right) + (down + up) + (before + after)
                out = stiff * (6.0 * mine - around) + spread
                applied[c, x, k] = out
                part = here * out
                curve = part if curve is None else curve + part
        curves.append(jnp.sum(curve, axis=0, keepdims=True))
    local_solve(applied, operator, solved)
    sums = restricted(basis, applied)
    whole = lane_sums(sums)
    primal[...] = whole
    stacked = jnp.concatenate([sums] + curves, axis=0)
    mine_row = lane_row(stacked)
    lane = lax.broadcasted_iota(jnp.int32, (48, 128), 1)
    sub = lax.broadcasted_iota(jnp.int32, (48, 128), 0)
    first = jnp.sum(jnp.where(lane == sub, primal_r[...], 0.0), axis=0, keepdims=True)
    row[...] = first + pltpu.roll(mine_row, 48, 1)
    for source, base in ((solved_r, 0), (solved, CASES)):
        low_x[base : base + CASES] = source[:, 0]
        high_x[base : base + CASES] = source[:, NX - 1]
        side_rows(source, low_y, 0, base * NX * COMP)
        side_rows(source, high_y, NY - 1, base * NX * COMP)


def steps_of(table, prior):
    total = jnp.sum(table[...], axis=0, keepdims=True)
    lane = lax.broadcasted_iota(jnp.int32, (1, 128), 1)
    steps = []
    for c in range(CASES):
        curvature = jnp.sum(jnp.where(lane == 96 + c, total, 0.0), axis=1, keepdims=True)
        steps.append(jnp.broadcast_to(prior[c] / curvature, (1, 128)))
    return steps


def smoothed_at(c, x, k, step, solved_r, solved_w, below_x, above_x, below_y, above_y, y_at):
    here = solved_r[c, x, k] - step * solved_w[c, x, k]
    at = (c * NX + x) * COMP + k
    under = below_y[at : at + 1, :] - step * below_y[TILES + at : TILES + at + 1, :]
    over = above_y[at : at + 1, :] - step * above_y[TILES + at : TILES + at + 1, :]
    beside = jnp.where(y_at == 0, jnp.broadcast_to(under, (NY, NZ)), 0.0)
    beside = beside + jnp.where(y_at == NY - 1, jnp.broadcast_to(over, (NY, NZ)), 0.0)
    if x == 0:
        beside = beside + (below_x[c, k] - step * below_x[CASES + c, k])
    if x == NX - 1:
        beside = beside + (above_x[c, k] - step * above_x[CASES + c, k])
    return here + 0.5 * beside


def coarse_kernel(
    prior, table, inverse, primal_r, primal_w, residual, applied, solved_r, solved_w,
    below_x, above_x, below_y, above_y,
    row, steps_out, coarse,
):
    steps = steps_of(table, prior)
    for c in range(CASES):
        steps_out[c : c + 1, :] = steps[c]
    lane = lax.broadcasted_iota(jnp.int32, (1, 128), 1)
    weight = jnp.zeros((1, 128), f32)
    for c in range(CASES):
        weight = jnp.where(lane // PRIMAL == c, steps[c], weight)
    everything = table[...]
    primal = everything - weight * pltpu.roll(everything, 80, 1)
    high, low = halves(primal)
    pair = jnp.concatenate([high, low], axis=1)
    source = lax.broadcasted_iota(jnp.int32, (256, LINE), 0) % 128
    target = lax.broadcasted_iota(jnp.int32, (256, LINE), 1)
    slot = lax.broadcasted_iota(jnp.int32, (8, LINE), 1) // PRIMAL
    rows = []
    for c in range(CASES):
        spread = jnp.where(source == c * PRIMAL + target % PRIMAL, 1.0, 0.0).astype(bf16)
        wide = mxu(pair, spread, NN)
        gathered = []
        for half in range(2):
            total = None
            for group in range(16):
                for z_high in range(2):
                    at = ((half * 16 + group) * 2 + z_high) * 8
                    part = jnp.where(slot == group * 2 + z_high, wide[at : at + 8], 0.0)
                    total = part if total is None else total + part
            gathered.append(total)
        for r in range(PRIMAL):
            total = None
            for half in range(2):
                part = gathered[half] * inverse[r, half]
                total = part if total is None else total + part
            folded = total[:, 0:128] + total[:, 128:256] + total[:, 256:384]
            rows.append(jnp.sum(folded, axis=0, keepdims=True))
    coarse_values = lane_sums(jnp.concatenate(rows, axis=0))
    coarse[...] = coarse_values

    y_at = lax.broadcasted_iota(jnp.int32, (NY, NZ), 0)
    sums = []
    for c in range(CASES):
        step = steps[c]
        total = None
        for x in range(NX):
            for k in range(COMP):
                smooth = smoothed_at(
                    c, x, k, step, solved_r, solved_w, below_x, above_x, below_y, above_y, y_at
                )
                part = (residual[c, x, k] - step * applied[c, x, k]) * smooth
                total = part if total is None else total + part
        own = primal_r[c * PRIMAL : (c + 1) * PRIMAL] - step * primal_w[c * PRIMAL : (c + 1) * PRIMAL]
        both = jnp.sum(own * coarse_values[c * PRIMAL : (c + 1) * PRIMAL], axis=0, keepdims=True)
        sums.append(
            jnp.sum(total, axis=0, keepdims=True) + jnp.where(lane == 0, both, 0.0)
        )
    row[...] = lane_row(jnp.concatenate(sums, axis=0))


def update_kernel(
    steps, coarse, basis, solution, residual, direction, applied, solved_r, solved_w,
    below_x, above_x, below_y, above_y,
    solution_next, residual_next, preconditioned,
):
    y_at = lax.broadcasted_iota(jnp.int32, (NY, NZ), 0)
    for c in range(CASES):
        step = steps[c : c + 1, :]
        for x in range(NX):
            for k in range(COMP):
                residual_next[c, x, k] = residual[c, x, k] - step * applied[c, x, k]
                solution_next[c, x, k] = solution[c, x, k] + step * direction[c, x, k]
                out = smoothed_at(
                    c, x, k, step, solved_r, solved_w, below_x, above_x, below_y, above_y, y_at
                )
                for p in range(NP):
                    at = c * PRIMAL + k * NP + p
                    out = out + basis[p, x] * coarse[at : at + 1, :]
                preconditioned[c, x, k] = out


def final_kernel(prior, parts, preconditioned, direction, direction_next, inner):
    total = jnp.sum(parts[...], axis=0, keepdims=True)
    inner[...] = total
    lane = lax.broadcasted_iota(jnp.int32, (1, 128), 1)
    for c in range(CASES):
        mine = jnp.sum(jnp.where(lane == c, total, 0.0), axis=1, keepdims=True)
        growth = jnp.broadcast_to(mine / prior[c], (1, NZ))
        for x in range(NX):
            for k in range(COMP):
                direction_next[c, x, k] = (
                    preconditioned[c, x, k] + growth * direction[c, x, k]
                )


VMEM = pl.BlockSpec(memory_space=pltpu.VMEM)
SMEM = pl.BlockSpec(memory_space=pltpu.SMEM)


def local_call(body, outs, scalars, *args):
    return pl.pallas_call(
        body,
        out_shape=[jax.ShapeDtypeStruct(shape, f32) for shape in outs],
        in_specs=[SMEM] * scalars + [VMEM] * (len(args) - scalars),
        out_specs=[VMEM] * len(outs),
        compiler_params=pltpu.CompilerParams(vmem_limit_bytes=40 << 20),
    )(*args)


def exchange(block, axes, count):
    spread = jnp.broadcast_to(block[None], (count,) + block.shape)
    return lax.all_to_all(spread, axes, 0, 0, tiled=True)


def neighbours(low, high, axes, count):
    up = [(i, i + 1) for i in range(count - 1)]
    down = [(i + 1, i) for i in range(count - 1)]
    return lax.ppermute(high, axes, up), lax.ppermute(low, axes, down)


def body(
    solution, residual, direction, stiffness, coupling, lower_factor, upper_factor,
    pivot_order, coarse_basis, coarse_inverse, inner_prior,
):
    solution, residual, direction = (
        a.transpose(0, 1, 3, 2, 4) for a in (solution, residual, direction)
    )
    end_x = (CASES, COMP, NY, NZ)
    end_y = (TILES, NZ)
    low_x, high_x, low_y, high_y = local_call(
        faces_kernel, [end_x, end_x, end_y, end_y], 0, direction, stiffness
    )
    below_y, above_y = neighbours(low_y, high_y, YZ_AXES, N_YZ)
    below_x, above_x = neighbours(low_x, high_x, GX_AXES, N_GX)

    operator, solved_r, primal_r = local_call(
        prepare_kernel, [(LINE, LINE), FIELD, (48, 128)], 0,
        residual, lower_factor[0, 0], upper_factor[0, 0], pivot_order[0], coarse_basis,
    )

    twice_x = (2 * CASES, COMP, NY, NZ)
    twice_y = (2 * TILES, NZ)
    applied, solved_w, primal_w, row, low_x, high_x, low_y, high_y = local_call(
        applied_kernel,
        [FIELD, FIELD, (48, 128), (1, 128), twice_x, twice_x, twice_y, twice_y], 0,
        direction, stiffness, coupling, below_x, above_x, below_y, above_y,
        coarse_basis, operator, solved_r, primal_r,
    )

    line = exchange(row, DEPTH, N_DEPTH)
    below_y, above_y = neighbours(low_y, high_y, YZ_AXES, N_YZ)
    below_x, above_x = neighbours(low_x, high_x, GX_AXES, N_GX)
    (inverse,) = local_call(
        by_depth_kernel, [(PRIMAL, 2, 8, LINE)], 0,
        coarse_inverse.reshape(PRIMAL * 48, 128),
    )
    table = exchange(line.reshape(N_DEPTH, 128), PLANE, N_PLANE)
    table = table.reshape(N_PLANE * N_DEPTH, 128)

    inner_row, steps, coarse = local_call(
        coarse_kernel, [(1, 128), (CASES, 128), (48, 128)], 1,
        inner_prior, table, inverse, primal_r, primal_w, residual, applied, solved_r, solved_w,
        below_x, above_x, below_y, above_y,
    )
    line = exchange(inner_row, DEPTH, N_DEPTH)
    solution_next, residual_next, preconditioned = local_call(
        update_kernel, [FIELD, FIELD, FIELD], 0,
        steps, coarse, coarse_basis, solution, residual, direction, applied,
        solved_r, solved_w, below_x, above_x, below_y, above_y,
    )
    parts = exchange(jnp.sum(line, axis=0), PLANE, N_PLANE)
    direction_next, inner = local_call(
        final_kernel, [FIELD, (1, 128)], 1,
        inner_prior, parts.reshape(N_PLANE, 128), preconditioned, direction,
    )
    solution_next, residual_next, direction_next = (
        a.transpose(0, 1, 3, 2, 4) for a in (solution_next, residual_next, direction_next)
    )
    return (solution_next, residual_next, direction_next, inner[0, :CASES])


def solution(mesh):
    fine = Mesh(mesh.devices.reshape(8, 4, 2, 4, 2), ("zl", "x", "c", "y", "zh"))
    field = P(None, GX_AXES, YZ_AXES, None, None)
    block = P(GX_AXES, YZ_AXES, None)
    factor = P(GX_AXES, YZ_AXES, None, None)
    in_specs = (
        field, field, field, block, block, factor, factor, block,
        P(None, GX_AXES, YZ_AXES, None), factor, P(),
    )
    return jax.shard_map(
        body,
        mesh=fine,
        in_specs=in_specs,
        out_specs=(field, field, field, P()),
        check_vma=False,
    )
```

```python
import jax
import jax.numpy as jnp
from jax import lax
from jax.experimental import pallas as pl
from jax.experimental.pallas import tpu as pltpu
from jax.sharding import Mesh, PartitionSpec as P


DEPTH = ("zh", "zl")
PLANE = ("x", "c", "y")
GX_AXES = ("zl", "x", "c")
YZ_AXES = ("y", "zh")
N_DEPTH = 16
N_PLANE = 32
N_GX = 64
N_YZ = 8

CASES, NX, COMP, NY, NZ = 4, 8, 3, 8, 128
NP = 4
PRIMAL = COMP * NP
LINE = COMP * NZ
TILES = CASES * NX * COMP
FIELD = (CASES, NX, COMP, NY, NZ)
f32 = jnp.float32
bf16 = jnp.bfloat16
NT = (((1,), (1,)), ((), ()))
NN = (((1,), (0,)), ((), ()))


def mxu(a, b, dims):
    return lax.dot_general(a, b, dims, preferred_element_type=f32)


def halves(a):
    high = a.astype(bf16)
    return high, (a - high.astype(f32)).astype(bf16)


def thirds(a):
    high = a.astype(bf16)
    rest = a - high.astype(f32)
    mid = rest.astype(bf16)
    return high, mid, (rest - mid.astype(f32)).astype(bf16)


def product(a, b, dims):
    a0, a1, a2 = thirds(a)
    b0, b1, b2 = thirds(b)
    small = mxu(a0, b2, dims) + mxu(a2, b0, dims) + mxu(a1, b1, dims)
    return (small + (mxu(a0, b1, dims) + mxu(a1, b0, dims))) + mxu(a0, b0, dims)


def product_of_halves(a, b, dims):
    a0, a1 = halves(a)
    b0, b1 = halves(b)
    return (mxu(a0, b1, dims) + mxu(a1, b0, dims)) + mxu(a0, b0, dims)


def picked(chosen, b, dims):
    high, low = halves(b)
    return mxu(chosen, low, dims) + mxu(chosen, high, dims)


def lane_sums(a):
    ones = jnp.ones((a.shape[1], 128), bf16)
    a0, a1, a2 = thirds(a)
    return (mxu(a2, ones, NN) + mxu(a1, ones, NN)) + mxu(a0, ones, NN)


def lane_row(a):
    rows = a.shape[0]
    if rows < 128:
        a = jnp.concatenate([a, jnp.zeros((128 - rows, 128), f32)], axis=0)
    ones = jnp.ones((8, 128), bf16)
    a0, a1, a2 = thirds(a)
    return ((mxu(ones, a2, NT) + mxu(ones, a1, NT)) + mxu(ones, a0, NT))[0:1]


def restricted(basis, field):
    rows = []
    for c in range(CASES):
        for k in range(COMP):
            for p in range(NP):
                total = basis[p, 0] * field[c, 0, k]
                for x in range(1, NX):
                    total = total + basis[p, x] * field[c, x, k]
                rows.append(jnp.sum(total, axis=0, keepdims=True))
    return jnp.concatenate(rows, axis=0)


def local_solve(field, operator_ref, out_ref):
    total = None
    for k in range(COMP):
        rows = field[:, :, k].reshape(CASES * NX * NY, NZ)
        part = product(rows, operator_ref[k * NZ : (k + 1) * NZ, :], NN)
        total = part if total is None else total + part
    for k in range(COMP):
        out_ref[:, :, k] = total[:, k * NZ : (k + 1) * NZ].reshape(CASES, NX, NY, NZ)


def side_rows(ref, out_ref, y, base):
    for c in range(CASES):
        for x in range(NX):
            for k in range(COMP):
                row = base + (c * NX + x) * COMP + k
                out_ref[row : row + 1, :] = ref[c, x, k, y : y + 1, :]


def faces_kernel(
    direction_hbm, stiffness_hbm, low_x, high_x, low_y, high_y, direction, stiffness, sems
):
    copies = [
        pltpu.make_async_copy(direction_hbm, direction, sems.at[0]),
        pltpu.make_async_copy(stiffness_hbm, stiffness, sems.at[1]),
    ]
    for copy in copies:
        copy.start()
    for copy in copies:
        copy.wait()
    for x, out in ((0, low_x), (NX - 1, high_x)):
        out[...] = direction[:, x] * stiffness[x][None, None]
    for y, out in ((0, low_y), (NY - 1, high_y)):
        for c in range(CASES):
            for x in range(NX):
                for k in range(COMP):
                    row = (c * NX + x) * COMP + k
                    out[row : row + 1, :] = (
                        direction[c, x, k, y : y + 1, :] * stiffness[x, y : y + 1, :]
                    )


def prepare_kernel(
    prior, residual, lower_hbm, upper_hbm, pivots_hbm, basis_hbm,
    operator, solved, primal, prior_rows,
    lower, upper, pivots, basis, sems,
):
    pairs = ((upper_hbm, upper), (lower_hbm, lower), (pivots_hbm, pivots), (basis_hbm, basis))
    copies = [
        pltpu.make_async_copy(source, target, sems.at[i])
        for i, (source, target) in enumerate(pairs)
    ]
    for copy in copies:
        copy.start()
    for c in range(CASES):
        prior_rows[c : c + 1, :] = jnp.full((1, 128), prior[c], f32)
    copies[0].wait()
    copies[1].wait()
    both = product_of_halves(upper[...], lower[...], NN)
    copies[2].wait()
    at = lax.broadcasted_iota(jnp.int32, (LINE, LINE), 0)
    chosen = jnp.where(at == pivots[...], 1.0, 0.0).astype(bf16)
    rows = picked(chosen, both, NN)
    operator[...] = picked(chosen, rows, NT)
    local_solve(residual, operator, solved)
    copies[3].wait()
    primal[...] = lane_sums(restricted(basis, residual))


def by_depth_kernel(inverse, by_depth):
    for r in range(PRIMAL):
        for half in range(2):
            for part in range(3):
                at = r * 48 + half * 3 + part
                by_depth[r, half, :, part * 128 : (part + 1) * 128] = inverse[
                    pl.ds(at, 8, stride=6), :
                ]


def applied_kernel(
    direction, stiffness, coupling, below_x, above_x, below_y, above_y,
    basis, operator, solved_r, primal_r,
    applied, solved, primal, row, low_x, high_x, low_y, high_y,
):
    y_at = lax.broadcasted_iota(jnp.int32, (NY, NZ), 0)
    z_at = lax.broadcasted_iota(jnp.int32, (NY, NZ), 1)
    first_y, last_y = y_at == 0, y_at == NY - 1
    first_z, last_z = z_at == 0, z_at == NZ - 1
    curves = []
    for c in range(CASES):
        curve = None
        for x in range(NX):
            stiff = stiffness[x]
            total = direction[c, x, 0] + direction[c, x, 1] + direction[c, x, 2]
            spread = coupling[x] * total
            for k in range(COMP):
                here = direction[c, x, k]
                mine = stiff * here
                left = below_x[c, k] if x == 0 else stiffness[x - 1] * direction[c, x - 1, k]
                right = above_x[c, k] if x == NX - 1 else stiffness[x + 1] * direction[c, x + 1, k]
                at = (c * NX + x) * COMP + k
                down = jnp.where(
                    first_y,
                    jnp.broadcast_to(below_y[at : at + 1, :], (NY, NZ)),
                    pltpu.roll(mine, 1, 0),
                )
                up = jnp.where(
                    last_y,
                    jnp.broadcast_to(above_y[at : at + 1, :], (NY, NZ)),
                    pltpu.roll(mine, NY - 1, 0),
                )
                before = jnp.where(first_z, 0.0, pltpu.roll(mine, 1, 1))
                after = jnp.where(last_z, 0.0, pltpu.roll(mine, NZ - 1, 1))
                around = (left + right) + (down + up) + (before + after)
                out = stiff * (6.0 * mine - around) + spread
                applied[c, x, k] = out
                part = here * out
                curve = part if curve is None else curve + part
        curves.append(jnp.sum(curve, axis=0, keepdims=True))
    local_solve(applied, operator, solved)
    sums = restricted(basis, applied)
    whole = lane_sums(sums)
    primal[...] = whole
    stacked = jnp.concatenate([sums] + curves, axis=0)
    mine_row = lane_row(stacked)
    lane = lax.broadcasted_iota(jnp.int32, (48, 128), 1)
    sub = lax.broadcasted_iota(jnp.int32, (48, 128), 0)
    first = jnp.sum(jnp.where(lane == sub, primal_r[...], 0.0), axis=0, keepdims=True)
    row[...] = jnp.broadcast_to((first + pltpu.roll(mine_row, 48, 1))[None], (N_DEPTH, 1, 128))
    for source, base in ((solved_r, 0), (solved, CASES)):
        low_x[base : base + CASES] = source[:, 0]
        high_x[base : base + CASES] = source[:, NX - 1]
        side_rows(source, low_y, 0, base * NX * COMP)
        side_rows(source, high_y, NY - 1, base * NX * COMP)


def steps_of(table, prior):
    total = jnp.sum(table[...], axis=0, keepdims=True)
    lane = lax.broadcasted_iota(jnp.int32, (1, 128), 1)
    steps = []
    for c in range(CASES):
        curvature = jnp.sum(jnp.where(lane == 96 + c, total, 0.0), axis=1, keepdims=True)
        steps.append(prior[c : c + 1, :] / jnp.broadcast_to(curvature, (1, 128)))
    return steps


def smoothed_at(c, x, k, step, solved_r, solved_w, below_x, above_x, below_y, above_y, y_at):
    here = solved_r[c, x, k] - step * solved_w[c, x, k]
    at = (c * NX + x) * COMP + k
    under = below_y[at : at + 1, :] - step * below_y[TILES + at : TILES + at + 1, :]
    over = above_y[at : at + 1, :] - step * above_y[TILES + at : TILES + at + 1, :]
    beside = jnp.where(y_at == 0, jnp.broadcast_to(under, (NY, NZ)), 0.0)
    beside = beside + jnp.where(y_at == NY - 1, jnp.broadcast_to(over, (NY, NZ)), 0.0)
    if x == 0:
        beside = beside + (below_x[c, k] - step * below_x[CASES + c, k])
    if x == NX - 1:
        beside = beside + (above_x[c, k] - step * above_x[CASES + c, k])
    return here + 0.5 * beside


def coarse_kernel(
    prior, table, inverse, primal_r, primal_w, residual, applied, solved_r, solved_w,
    below_x, above_x, below_y, above_y,
    row, steps_out, coarse,
):
    steps = steps_of(table, prior)
    for c in range(CASES):
        steps_out[c : c + 1, :] = steps[c]
    lane = lax.broadcasted_iota(jnp.int32, (1, 128), 1)
    weight = jnp.zeros((1, 128), f32)
    for c in range(CASES):
        weight = jnp.where(lane // PRIMAL == c, steps[c], weight)
    everything = table[...]
    primal = everything - weight * pltpu.roll(everything, 80, 1)
    high, low = halves(primal)
    pair = jnp.concatenate([high, low], axis=1)
    source = lax.broadcasted_iota(jnp.int32, (256, LINE), 0) % 128
    target = lax.broadcasted_iota(jnp.int32, (256, LINE), 1)
    slot = lax.broadcasted_iota(jnp.int32, (8, LINE), 1) // PRIMAL
    rows = []
    for c in range(CASES):
        spread = jnp.where(source == c * PRIMAL + target % PRIMAL, 1.0, 0.0).astype(bf16)
        wide = mxu(pair, spread, NN)
        gathered = []
        for half in range(2):
            total = None
            for group in range(16):
                for z_high in range(2):
                    at = ((half * 16 + group) * 2 + z_high) * 8
                    part = jnp.where(slot == group * 2 + z_high, wide[at : at + 8], 0.0)
                    total = part if total is None else total + part
            gathered.append(total)
        for r in range(PRIMAL):
            total = None
            for half in range(2):
                part = gathered[half] * inverse[r, half]
                total = part if total is None else total + part
            folded = total[:, 0:128] + total[:, 128:256] + total[:, 256:384]
            rows.append(jnp.sum(folded, axis=0, keepdims=True))
    coarse_values = lane_sums(jnp.concatenate(rows, axis=0))
    coarse[...] = coarse_values

    y_at = lax.broadcasted_iota(jnp.int32, (NY, NZ), 0)
    sums = []
    for c in range(CASES):
        step = steps[c]
        total = None
        for x in range(NX):
            for k in range(COMP):
                smooth = smoothed_at(
                    c, x, k, step, solved_r, solved_w, below_x, above_x, below_y, above_y, y_at
                )
                part = (residual[c, x, k] - step * applied[c, x, k]) * smooth
                total = part if total is None else total + part
        own = primal_r[c * PRIMAL : (c + 1) * PRIMAL] - step * primal_w[c * PRIMAL : (c + 1) * PRIMAL]
        both = jnp.sum(own * coarse_values[c * PRIMAL : (c + 1) * PRIMAL], axis=0, keepdims=True)
        sums.append(
            jnp.sum(total, axis=0, keepdims=True) + jnp.where(lane == 0, both, 0.0)
        )
    row[...] = jnp.broadcast_to(
        lane_row(jnp.concatenate(sums, axis=0))[None], (N_DEPTH, 1, 128)
    )


def advance_kernel(
    steps, solution, residual, direction, applied, solution_next, residual_next
):
    for c in range(CASES):
        step = steps[c : c + 1, :]
        for x in range(NX):
            for k in range(COMP):
                residual_next[c, x, k] = residual[c, x, k] - step * applied[c, x, k]
                solution_next[c, x, k] = solution[c, x, k] + step * direction[c, x, k]


def precondition_kernel(
    steps, coarse, basis, solved_r, solved_w, below_x, above_x, below_y, above_y, preconditioned
):
    y_at = lax.broadcasted_iota(jnp.int32, (NY, NZ), 0)
    for c in range(CASES):
        step = steps[c : c + 1, :]
        for x in range(NX):
            for k in range(COMP):
                out = smoothed_at(
                    c, x, k, step, solved_r, solved_w, below_x, above_x, below_y, above_y, y_at
                )
                for p in range(NP):
                    at = c * PRIMAL + k * NP + p
                    out = out + basis[p, x] * coarse[at : at + 1, :]
                preconditioned[c, x, k] = out


def final_kernel(prior, parts, preconditioned, direction, direction_next, inner):
    total = jnp.sum(parts[...], axis=0, keepdims=True)
    inner[...] = total[0, :CASES]
    lane = lax.broadcasted_iota(jnp.int32, (1, 128), 1)
    for c in range(CASES):
        mine = jnp.sum(jnp.where(lane == c, total, 0.0), axis=1, keepdims=True)
        growth = jnp.broadcast_to(mine, (1, NZ)) / prior[c : c + 1, :]
        for x in range(NX):
            for k in range(COMP):
                direction_next[c, x, k] = (
                    preconditioned[c, x, k] + growth * direction[c, x, k]
                )


VMEM = pl.BlockSpec(memory_space=pltpu.VMEM)
SMEM = pl.BlockSpec(memory_space=pltpu.SMEM)
HBM = pl.BlockSpec(memory_space=pltpu.HBM)


def local_call(body, outs, spaces, *args, scratch=()):
    specs = [{"s": SMEM, "v": VMEM, "h": HBM}[space] for space in spaces]
    specs += [VMEM] * (len(args) - len(specs))
    args = tuple(
        pltpu.with_memory_space_constraint(arg, pltpu.HBM) if spec is HBM else arg
        for arg, spec in zip(args, specs)
    )
    return pl.pallas_call(
        body,
        out_shape=[jax.ShapeDtypeStruct(shape, f32) for shape in outs],
        in_specs=specs,
        out_specs=[VMEM] * len(outs),
        scratch_shapes=list(scratch),
        compiler_params=pltpu.CompilerParams(vmem_limit_bytes=20 << 20),
    )(*args)


def spread(block, count):
    return jnp.broadcast_to(block[None], (count,) + block.shape)


def exchange(rows, axes):
    return lax.all_to_all(rows, axes, 0, 0, tiled=True)


def neighbours(low, high, axes, count):
    up = [(i, i + 1) for i in range(count - 1)]
    down = [(i + 1, i) for i in range(count - 1)]
    return lax.ppermute(high, axes, up), lax.ppermute(low, axes, down)


def body(
    solution, residual, direction, stiffness, coupling, lower_factor, upper_factor,
    pivot_order, coarse_basis, coarse_inverse, inner_prior,
):
    solution, residual, direction = (
        a.transpose(0, 1, 3, 2, 4) for a in (solution, residual, direction)
    )
    end_x = (CASES, COMP, NY, NZ)
    end_y = (TILES, NZ)
    low_x, high_x, low_y, high_y = local_call(
        faces_kernel, [end_x, end_x, end_y, end_y], "hh", direction, stiffness,
        scratch=[
            pltpu.VMEM(FIELD, f32), pltpu.VMEM((NX, NY, NZ), f32), pltpu.SemaphoreType.DMA((2,)),
        ],
    )
    below_y, above_y = neighbours(low_y, high_y, YZ_AXES, N_YZ)
    below_x, above_x = neighbours(low_x, high_x, GX_AXES, N_GX)

    operator, solved_r, primal_r, prior_rows = local_call(
        prepare_kernel, [(LINE, LINE), FIELD, (48, 128), (CASES, 128)], "svhhhh",
        inner_prior, residual, lower_factor[0, 0], upper_factor[0, 0], pivot_order[0],
        coarse_basis,
        scratch=[
            pltpu.VMEM((LINE, LINE), f32), pltpu.VMEM((LINE, LINE), f32),
            pltpu.VMEM((1, LINE), jnp.int32), pltpu.VMEM((NP, NX, NY, NZ), f32),
            pltpu.SemaphoreType.DMA((4,)),
        ],
    )

    twice_x = (2 * CASES, COMP, NY, NZ)
    twice_y = (2 * TILES, NZ)
    rows_z = (N_DEPTH, 1, 128)
    applied, solved_w, primal_w, rows, low_x, high_x, low_y, high_y = local_call(
        applied_kernel,
        [FIELD, FIELD, (48, 128), rows_z, twice_x, twice_x, twice_y, twice_y], "",
        direction, stiffness, coupling, below_x, above_x, below_y, above_y,
        coarse_basis, operator, solved_r, primal_r,
    )

    line = exchange(rows, DEPTH)
    below_y, above_y = neighbours(low_y, high_y, YZ_AXES, N_YZ)
    below_x, above_x = neighbours(low_x, high_x, GX_AXES, N_GX)
    (inverse,) = local_call(
        by_depth_kernel, [(PRIMAL, 2, 8, LINE)], "",
        coarse_inverse.reshape(PRIMAL * 48, 128),
    )
    table = exchange(spread(line.reshape(N_DEPTH, 128), N_PLANE), PLANE)
    table = table.reshape(N_PLANE * N_DEPTH, 128)

    halo = (below_x, above_x, below_y, above_y)
    rows, steps, coarse = local_call(
        coarse_kernel, [rows_z, (CASES, 128), (48, 128)], "",
        prior_rows, table, inverse, primal_r, primal_w, residual, applied, solved_r, solved_w,
        *halo,
    )
    line = exchange(rows, DEPTH)
    solution_next, residual_next = local_call(
        advance_kernel, [FIELD, FIELD], "",
        steps, solution, residual, direction, applied,
    )
    parts = exchange(spread(jnp.sum(line, axis=0), N_PLANE), PLANE)
    (preconditioned,) = local_call(
        precondition_kernel, [FIELD], "",
        steps, coarse, coarse_basis, solved_r, solved_w, *halo,
    )
    direction_next, inner = local_call(
        final_kernel, [FIELD, (CASES,)], "",
        prior_rows, parts.reshape(N_PLANE, 128), preconditioned, direction,
    )
    solution_next, residual_next, direction_next = (
        a.transpose(0, 1, 3, 2, 4) for a in (solution_next, residual_next, direction_next)
    )
    return (solution_next, residual_next, direction_next, inner)


def solution(mesh):
    fine = Mesh(mesh.devices.reshape(8, 4, 2, 4, 2), ("zl", "x", "c", "y", "zh"))
    field = P(None, GX_AXES, YZ_AXES, None, None)
    block = P(GX_AXES, YZ_AXES, None)
    factor = P(GX_AXES, YZ_AXES, None, None)
    in_specs = (
        field, field, field, block, block, factor, factor, block,
        P(None, GX_AXES, YZ_AXES, None), factor, P(),
    )
    return jax.shard_map(
        body,
        mesh=fine,
        in_specs=in_specs,
        out_specs=(field, field, field, P()),
        check_vma=False,
    )
```

```python
import jax
import jax.numpy as jnp
from jax import lax
from jax.experimental import pallas as pl
from jax.experimental.pallas import tpu as pltpu
from jax.sharding import Mesh, PartitionSpec as P


DEPTH = ("zh", "zl")
PLANE = ("x", "c", "y")
GX_AXES = ("zl", "x", "c")
YZ_AXES = ("y", "zh")
N_DEPTH = 16
N_PLANE = 32
N_GX = 64
N_YZ = 8

CASES, NX, COMP, NY, NZ = 4, 8, 3, 8, 128
NP = 4
PRIMAL = COMP * NP
LINE = COMP * NZ
TILES = CASES * NX * COMP
FIELD = (CASES, NX, COMP, NY, NZ)
f32 = jnp.float32
bf16 = jnp.bfloat16
OPERATOR = jax.ShapeDtypeStruct((2 * LINE, LINE), bf16)
NT = (((1,), (1,)), ((), ()))
NN = (((1,), (0,)), ((), ()))


def mxu(a, b, dims):
    return lax.dot_general(a, b, dims, preferred_element_type=f32)


def halves(a):
    high = a.astype(bf16)
    return high, (a - high.astype(f32)).astype(bf16)


def thirds(a):
    high = a.astype(bf16)
    rest = a - high.astype(f32)
    mid = rest.astype(bf16)
    return high, mid, (rest - mid.astype(f32)).astype(bf16)


def product_of_halves(a, b):
    a0, a1 = halves(a)
    b0, b1 = halves(b)
    return mxu(
        jnp.concatenate([a0, a0, a1], axis=1), jnp.concatenate([b0, b1, b0], axis=0), NN
    )


def lane_sums(a):
    ones = jnp.ones((a.shape[1], 128), bf16)
    a0, a1, a2 = thirds(a)
    return (mxu(a2, ones, NN) + mxu(a1, ones, NN)) + mxu(a0, ones, NN)


def lane_row(a):
    rows = a.shape[0]
    if rows < 128:
        a = jnp.concatenate([a, jnp.zeros((128 - rows, 128), f32)], axis=0)
    ones = jnp.ones((8, 128), bf16)
    a0, a1, a2 = thirds(a)
    return ((mxu(ones, a2, NT) + mxu(ones, a1, NT)) + mxu(ones, a0, NT))[0:1]


def restricted(basis, field):
    rows = []
    for c in range(CASES):
        for k in range(COMP):
            for p in range(NP):
                total = basis[p, 0] * field[c, 0, k]
                for x in range(1, NX):
                    total = total + basis[p, x] * field[c, x, k]
                rows.append(jnp.sum(total, axis=0, keepdims=True))
    return jnp.concatenate(rows, axis=0)


def local_solve(field, operator, out_ref):
    rows = [field[:, :, k].reshape(CASES * NX * NY, NZ) for k in range(COMP)]
    parts = [thirds(row) for row in rows]
    high, mid, low = (jnp.concatenate([part[i] for part in parts], axis=1) for i in range(3))
    whole = operator[...]
    first, second = whole[:LINE], whole[LINE:]
    total = mxu(
        jnp.concatenate([low, mid, high, mid, high], axis=1),
        jnp.concatenate([first, second, second, first, first], axis=0),
        NN,
    )
    for k in range(COMP):
        out_ref[:, :, k] = total[:, k * NZ : (k + 1) * NZ].reshape(CASES, NX, NY, NZ)


def side_rows(ref, out_ref, y, base):
    flat = ref.reshape(TILES * NY, NZ)
    for at in range(0, TILES, 8):
        out_ref[base + at : base + at + 8, :] = flat[pl.ds(at * NY + y, 8, stride=NY), :]


def faces_kernel(
    direction_hbm, stiffness_hbm, low_x, high_x, low_y, high_y, direction, stiffness, sems
):
    copies = [
        pltpu.make_async_copy(direction_hbm, direction, sems.at[0]),
        pltpu.make_async_copy(stiffness_hbm, stiffness, sems.at[1]),
    ]
    for copy in copies:
        copy.start()
    for copy in copies:
        copy.wait()
    for x, out in ((0, low_x), (NX - 1, high_x)):
        out[...] = direction[:, x] * stiffness[x][None, None]
    for y, out in ((0, low_y), (NY - 1, high_y)):
        for c in range(CASES):
            for x in range(NX):
                for k in range(COMP):
                    row = (c * NX + x) * COMP + k
                    out[row : row + 1, :] = (
                        direction[c, x, k, y : y + 1, :] * stiffness[x, y : y + 1, :]
                    )


def prepare_kernel(
    residual, lower_hbm, upper_hbm, pivots_hbm, basis_hbm, prior_hbm,
    operator, solved, primal, prior_rows,
    lower, upper, pivots, basis, prior, sems,
):
    pairs = (
        (upper_hbm, upper), (lower_hbm, lower), (pivots_hbm, pivots), (basis_hbm, basis),
        (prior_hbm, prior),
    )
    copies = [
        pltpu.make_async_copy(source, target, sems.at[i])
        for i, (source, target) in enumerate(pairs)
    ]
    for copy in copies:
        copy.start()
    for copy in copies:
        copy.wait()
    for c in range(CASES):
        prior_rows[c : c + 1, :] = jnp.broadcast_to(prior[0:1, c : c + 1], (1, 128))
    both = jnp.concatenate(halves(product_of_halves(upper[...], lower[...])), axis=1)
    at = lax.broadcasted_iota(jnp.int32, (LINE, LINE), 0)
    chosen = jnp.where(at == pivots[...], 1.0, 0.0).astype(bf16)
    rows = mxu(chosen, both, NN).astype(bf16)
    rows = jnp.concatenate([rows[:, :LINE], rows[:, LINE:]], axis=0)
    picked = mxu(chosen, rows, NT).astype(bf16)
    operator[:LINE, :] = picked[:, :LINE]
    operator[LINE:, :] = picked[:, LINE:]
    local_solve(residual, operator, solved)
    primal[...] = lane_sums(restricted(basis, residual))


def by_depth_kernel(inverse, by_depth):
    for r in range(PRIMAL):
        for half in range(2):
            for part in range(3):
                at = r * 48 + half * 3 + part
                by_depth[r, half, :, part * 128 : (part + 1) * 128] = inverse[
                    pl.ds(at, 8, stride=6), :
                ]


def applied_kernel(
    direction, stiffness, coupling, below_x, above_x, below_y, above_y,
    basis, operator, solved_r, primal_r,
    applied, solved, primal, row, low_x, high_x, low_y, high_y,
):
    y_at = lax.broadcasted_iota(jnp.int32, (NY, NZ), 0)
    z_at = lax.broadcasted_iota(jnp.int32, (NY, NZ), 1)
    first_y, last_y = y_at == 0, y_at == NY - 1
    first_z, last_z = z_at == 0, z_at == NZ - 1
    curves = []
    for c in range(CASES):
        curve = None
        for x in range(NX):
            stiff = stiffness[x]
            total = direction[c, x, 0] + direction[c, x, 1] + direction[c, x, 2]
            spread = coupling[x] * total
            for k in range(COMP):
                here = direction[c, x, k]
                mine = stiff * here
                left = below_x[c, k] if x == 0 else stiffness[x - 1] * direction[c, x - 1, k]
                right = above_x[c, k] if x == NX - 1 else stiffness[x + 1] * direction[c, x + 1, k]
                at = (c * NX + x) * COMP + k
                down = jnp.where(
                    first_y,
                    jnp.broadcast_to(below_y[at : at + 1, :], (NY, NZ)),
                    pltpu.roll(mine, 1, 0),
                )
                up = jnp.where(
                    last_y,
                    jnp.broadcast_to(above_y[at : at + 1, :], (NY, NZ)),
                    pltpu.roll(mine, NY - 1, 0),
                )
                before = jnp.where(first_z, 0.0, pltpu.roll(mine, 1, 1))
                after = jnp.where(last_z, 0.0, pltpu.roll(mine, NZ - 1, 1))
                around = (left + right) + (down + up) + (before + after)
                out = stiff * (6.0 * mine - around) + spread
                applied[c, x, k] = out
                part = here * out
                curve = part if curve is None else curve + part
        curves.append(jnp.sum(curve, axis=0, keepdims=True))
    local_solve(applied, operator, solved)
    sums = restricted(basis, applied)
    whole = lane_sums(sums)
    primal[...] = whole
    stacked = jnp.concatenate([sums] + curves, axis=0)
    mine_row = lane_row(stacked)
    lane = lax.broadcasted_iota(jnp.int32, (48, 128), 1)
    sub = lax.broadcasted_iota(jnp.int32, (48, 128), 0)
    first = jnp.sum(jnp.where(lane == sub, primal_r[...], 0.0), axis=0, keepdims=True)
    row[...] = jnp.broadcast_to((first + pltpu.roll(mine_row, 48, 1))[None], (N_DEPTH, 1, 128))
    for source, base in ((solved_r, 0), (solved, CASES)):
        low_x[base : base + CASES] = source[:, 0]
        high_x[base : base + CASES] = source[:, NX - 1]
        side_rows(source, low_y, 0, base * NX * COMP)
        side_rows(source, high_y, NY - 1, base * NX * COMP)


def steps_of(table, prior):
    total = jnp.sum(table[...], axis=0, keepdims=True)
    lane = lax.broadcasted_iota(jnp.int32, (1, 128), 1)
    steps = []
    for c in range(CASES):
        curvature = jnp.sum(jnp.where(lane == 96 + c, total, 0.0), axis=1, keepdims=True)
        steps.append(prior[c : c + 1, :] / jnp.broadcast_to(curvature, (1, 128)))
    return steps


def smoothed_at(c, x, k, step, solved_r, solved_w, below_x, above_x, below_y, above_y, y_at):
    here = solved_r[c, x, k] - step * solved_w[c, x, k]
    at = (c * NX + x) * COMP + k
    under = below_y[at : at + 1, :] - step * below_y[TILES + at : TILES + at + 1, :]
    over = above_y[at : at + 1, :] - step * above_y[TILES + at : TILES + at + 1, :]
    beside = jnp.where(y_at == 0, jnp.broadcast_to(under, (NY, NZ)), 0.0)
    beside = beside + jnp.where(y_at == NY - 1, jnp.broadcast_to(over, (NY, NZ)), 0.0)
    if x == 0:
        beside = beside + (below_x[c, k] - step * below_x[CASES + c, k])
    if x == NX - 1:
        beside = beside + (above_x[c, k] - step * above_x[CASES + c, k])
    return here + 0.5 * beside


def coarse_kernel(
    prior, table, inverse, primal_r, primal_w, residual, applied, solved_r, solved_w,
    below_x, above_x, below_y, above_y,
    row, steps_out, coarse,
):
    steps = steps_of(table, prior)
    for c in range(CASES):
        steps_out[c : c + 1, :] = steps[c]
    lane = lax.broadcasted_iota(jnp.int32, (1, 128), 1)
    weight = jnp.zeros((1, 128), f32)
    for c in range(CASES):
        weight = jnp.where(lane // PRIMAL == c, steps[c], weight)
    everything = table[...]
    primal = everything - weight * pltpu.roll(everything, 80, 1)
    high, low = halves(primal)
    pair = jnp.concatenate([high, low], axis=1)
    source = lax.broadcasted_iota(jnp.int32, (128, LINE), 0)
    target = lax.broadcasted_iota(jnp.int32, (128, LINE), 1) % PRIMAL
    slot = lax.broadcasted_iota(jnp.int32, (8, LINE), 1) // PRIMAL
    rows = []
    for c in range(CASES):
        spread = jnp.where(source == c * PRIMAL + target, 1.0, 0.0).astype(bf16)
        wide = mxu(pair, jnp.concatenate([spread, spread], axis=0), NN)
        gathered = []
        for half in range(2):
            total = None
            for group in range(16):
                for z_high in range(2):
                    at = ((half * 16 + group) * 2 + z_high) * 8
                    part = jnp.where(slot == group * 2 + z_high, wide[at : at + 8], 0.0)
                    total = part if total is None else total + part
            gathered.append(total)
        for r in range(PRIMAL):
            total = None
            for half in range(2):
                part = gathered[half] * inverse[r, half]
                total = part if total is None else total + part
            folded = total[:, 0:128] + total[:, 128:256] + total[:, 256:384]
            rows.append(jnp.sum(folded, axis=0, keepdims=True))
    coarse_values = lane_sums(jnp.concatenate(rows, axis=0))
    coarse[...] = coarse_values

    y_at = lax.broadcasted_iota(jnp.int32, (NY, NZ), 0)
    sums = []
    for c in range(CASES):
        step = steps[c]
        total = None
        for x in range(NX):
            for k in range(COMP):
                smooth = smoothed_at(
                    c, x, k, step, solved_r, solved_w, below_x, above_x, below_y, above_y, y_at
                )
                part = (residual[c, x, k] - step * applied[c, x, k]) * smooth
                total = part if total is None else total + part
        own = primal_r[c * PRIMAL : (c + 1) * PRIMAL] - step * primal_w[c * PRIMAL : (c + 1) * PRIMAL]
        both = jnp.sum(own * coarse_values[c * PRIMAL : (c + 1) * PRIMAL], axis=0, keepdims=True)
        sums.append(
            jnp.sum(total, axis=0, keepdims=True) + jnp.where(lane == 0, both, 0.0)
        )
    row[...] = jnp.broadcast_to(
        lane_row(jnp.concatenate(sums, axis=0))[None], (N_DEPTH, 1, 128)
    )


def advance_kernel(
    steps, solution, residual, direction, applied, solution_next, residual_next
):
    for c in range(CASES):
        step = steps[c : c + 1, :]
        for x in range(NX):
            for k in range(COMP):
                residual_next[c, x, k] = residual[c, x, k] - step * applied[c, x, k]
                solution_next[c, x, k] = solution[c, x, k] + step * direction[c, x, k]


def precondition_kernel(
    steps, coarse, basis, solved_r, solved_w, below_x, above_x, below_y, above_y, preconditioned
):
    y_at = lax.broadcasted_iota(jnp.int32, (NY, NZ), 0)
    for c in range(CASES):
        step = steps[c : c + 1, :]
        for x in range(NX):
            for k in range(COMP):
                out = smoothed_at(
                    c, x, k, step, solved_r, solved_w, below_x, above_x, below_y, above_y, y_at
                )
                for p in range(NP):
                    at = c * PRIMAL + k * NP + p
                    out = out + basis[p, x] * coarse[at : at + 1, :]
                preconditioned[c, x, k] = out


def final_kernel(prior, parts, preconditioned, direction, direction_next, inner):
    total = jnp.sum(parts[...], axis=0, keepdims=True)
    inner[...] = total[0, :CASES]
    lane = lax.broadcasted_iota(jnp.int32, (1, 128), 1)
    for c in range(CASES):
        mine = jnp.sum(jnp.where(lane == c, total, 0.0), axis=1, keepdims=True)
        growth = jnp.broadcast_to(mine, (1, NZ)) / prior[c : c + 1, :]
        for x in range(NX):
            for k in range(COMP):
                direction_next[c, x, k] = (
                    preconditioned[c, x, k] + growth * direction[c, x, k]
                )


VMEM = pl.BlockSpec(memory_space=pltpu.VMEM)
HBM = pl.BlockSpec(memory_space=pltpu.HBM)


def local_call(body, outs, spaces, *args, scratch=()):
    specs = [{"v": VMEM, "h": HBM}[space] for space in spaces]
    specs += [VMEM] * (len(args) - len(specs))
    args = tuple(
        pltpu.with_memory_space_constraint(arg, pltpu.HBM) if spec is HBM else arg
        for arg, spec in zip(args, specs)
    )
    return pl.pallas_call(
        body,
        out_shape=[
            shape if hasattr(shape, "dtype") else jax.ShapeDtypeStruct(shape, f32)
            for shape in outs
        ],
        in_specs=specs,
        out_specs=[VMEM] * len(outs),
        scratch_shapes=list(scratch),
        compiler_params=pltpu.CompilerParams(vmem_limit_bytes=20 << 20),
    )(*args)


def spread(block, count):
    return jnp.broadcast_to(block[None], (count,) + block.shape)


def exchange(rows, axes):
    return lax.all_to_all(rows, axes, 0, 0, tiled=True)


def neighbours(low, high, axes, count):
    up = [(i, i + 1) for i in range(count - 1)]
    down = [(i + 1, i) for i in range(count - 1)]
    return lax.ppermute(high, axes, up), lax.ppermute(low, axes, down)


def body(
    solution, residual, direction, stiffness, coupling, lower_factor, upper_factor,
    pivot_order, coarse_basis, coarse_inverse, inner_prior,
):
    solution, residual, direction = (
        a.transpose(0, 1, 3, 2, 4) for a in (solution, residual, direction)
    )
    end_x = (CASES, COMP, NY, NZ)
    end_y = (TILES, NZ)
    low_x, high_x, low_y, high_y = local_call(
        faces_kernel, [end_x, end_x, end_y, end_y], "hh", direction, stiffness,
        scratch=[
            pltpu.VMEM(FIELD, f32), pltpu.VMEM((NX, NY, NZ), f32), pltpu.SemaphoreType.DMA((2,)),
        ],
    )
    below_y, above_y = neighbours(low_y, high_y, YZ_AXES, N_YZ)
    below_x, above_x = neighbours(low_x, high_x, GX_AXES, N_GX)

    operator, solved_r, primal_r, prior_rows = local_call(
        prepare_kernel, [OPERATOR, FIELD, (48, 128), (CASES, 128)], "vhhhhh",
        residual, lower_factor[0, 0], upper_factor[0, 0], pivot_order[0], coarse_basis,
        inner_prior.reshape(1, CASES),
        scratch=[
            pltpu.VMEM((LINE, LINE), f32), pltpu.VMEM((LINE, LINE), f32),
            pltpu.VMEM((1, LINE), jnp.int32), pltpu.VMEM((NP, NX, NY, NZ), f32),
            pltpu.VMEM((1, CASES), f32), pltpu.SemaphoreType.DMA((5,)),
        ],
    )

    twice_x = (2 * CASES, COMP, NY, NZ)
    twice_y = (2 * TILES, NZ)
    rows_z = (N_DEPTH, 1, 128)
    applied, solved_w, primal_w, rows, low_x, high_x, low_y, high_y = local_call(
        applied_kernel,
        [FIELD, FIELD, (48, 128), rows_z, twice_x, twice_x, twice_y, twice_y], "",
        direction, stiffness, coupling, below_x, above_x, below_y, above_y,
        coarse_basis, operator, solved_r, primal_r,
    )

    line = exchange(rows, DEPTH)
    below_y, above_y = neighbours(low_y, high_y, YZ_AXES, N_YZ)
    below_x, above_x = neighbours(low_x, high_x, GX_AXES, N_GX)
    (inverse,) = local_call(
        by_depth_kernel, [(PRIMAL, 2, 8, LINE)], "",
        coarse_inverse.reshape(PRIMAL * 48, 128),
    )
    table = exchange(spread(line.reshape(N_DEPTH, 128), N_PLANE), PLANE)
    table = table.reshape(N_PLANE * N_DEPTH, 128)

    halo = (below_x, above_x, below_y, above_y)
    rows, steps, coarse = local_call(
        coarse_kernel, [rows_z, (CASES, 128), (48, 128)], "",
        prior_rows, table, inverse, primal_r, primal_w, residual, applied, solved_r, solved_w,
        *halo,
    )
    line = exchange(rows, DEPTH)
    solution_next, residual_next = local_call(
        advance_kernel, [FIELD, FIELD], "",
        steps, solution, residual, direction, applied,
    )
    parts = exchange(spread(jnp.sum(line, axis=0), N_PLANE), PLANE)
    (preconditioned,) = local_call(
        precondition_kernel, [FIELD], "",
        steps, coarse, coarse_basis, solved_r, solved_w, *halo,
    )
    direction_next, inner = local_call(
        final_kernel, [FIELD, (CASES,)], "",
        prior_rows, parts.reshape(N_PLANE, 128), preconditioned, direction,
    )
    solution_next, residual_next, direction_next = (
        a.transpose(0, 1, 3, 2, 4) for a in (solution_next, residual_next, direction_next)
    )
    return (solution_next, residual_next, direction_next, inner)


def solution(mesh):
    fine = Mesh(mesh.devices.reshape(8, 4, 2, 4, 2), ("zl", "x", "c", "y", "zh"))
    field = P(None, GX_AXES, YZ_AXES, None, None)
    block = P(GX_AXES, YZ_AXES, None)
    factor = P(GX_AXES, YZ_AXES, None, None)
    in_specs = (
        field, field, field, block, block, factor, factor, block,
        P(None, GX_AXES, YZ_AXES, None), factor, P(),
    )
    return jax.shard_map(
        body,
        mesh=fine,
        in_specs=in_specs,
        out_specs=(field, field, field, P()),
        check_vma=False,
    )
```

```python
import jax
import jax.numpy as jnp
from jax import lax
from jax.experimental import pallas as pl
from jax.experimental.pallas import tpu as pltpu
from jax.sharding import Mesh, PartitionSpec as P


DEPTH = ("zh", "zl")
PLANE = ("x", "c", "y")
GX_AXES = ("zl", "x", "c")
YZ_AXES = ("y", "zh")
N_DEPTH = 16
N_PLANE = 32
N_GX = 64
N_YZ = 8

CASES, NX, COMP, NY, NZ = 4, 8, 3, 8, 128
NP = 4
PRIMAL = COMP * NP
LINE = COMP * NZ
TILES = CASES * NX * COMP
FIELD = (CASES, NX, COMP, NY, NZ)
f32 = jnp.float32
bf16 = jnp.bfloat16
OPERATOR = jax.ShapeDtypeStruct((2 * LINE, LINE), bf16)
NT = (((1,), (1,)), ((), ()))
NN = (((1,), (0,)), ((), ()))


def mxu(a, b, dims):
    return lax.dot_general(a, b, dims, preferred_element_type=f32)


def halves(a):
    high = a.astype(bf16)
    return high, (a - high.astype(f32)).astype(bf16)


def thirds(a):
    high = a.astype(bf16)
    rest = a - high.astype(f32)
    mid = rest.astype(bf16)
    return high, mid, (rest - mid.astype(f32)).astype(bf16)


def product_of_halves(a, b):
    a0, a1 = halves(a)
    b0, b1 = halves(b)
    return mxu(
        jnp.concatenate([a0, a0, a1], axis=1), jnp.concatenate([b0, b1, b0], axis=0), NN
    )


def lane_sums(a):
    ones = jnp.ones((a.shape[1], 128), bf16)
    a0, a1, a2 = thirds(a)
    return (mxu(a2, ones, NN) + mxu(a1, ones, NN)) + mxu(a0, ones, NN)


def lane_row(a):
    rows = a.shape[0]
    if rows < 128:
        a = jnp.concatenate([a, jnp.zeros((128 - rows, 128), f32)], axis=0)
    ones = jnp.ones((8, 128), bf16)
    a0, a1, a2 = thirds(a)
    return ((mxu(ones, a2, NT) + mxu(ones, a1, NT)) + mxu(ones, a0, NT))[0:1]


def restricted(basis, field):
    rows = []
    for c in range(CASES):
        for k in range(COMP):
            for p in range(NP):
                total = basis[p, 0] * field[c, 0, k]
                for x in range(1, NX):
                    total = total + basis[p, x] * field[c, x, k]
                rows.append(jnp.sum(total, axis=0, keepdims=True))
    return jnp.concatenate(rows, axis=0)


def local_solve(field, operator, out_ref):
    rows = [field[:, :, k].reshape(CASES * NX * NY, NZ) for k in range(COMP)]
    parts = [thirds(row) for row in rows]
    high, mid, low = (jnp.concatenate([part[i] for part in parts], axis=1) for i in range(3))
    whole = operator[...]
    first, second = whole[:LINE], whole[LINE:]
    total = mxu(
        jnp.concatenate([low, mid, high, mid, high], axis=1),
        jnp.concatenate([first, second, second, first, first], axis=0),
        NN,
    )
    for k in range(COMP):
        out_ref[:, :, k] = total[:, k * NZ : (k + 1) * NZ].reshape(CASES, NX, NY, NZ)


def side_rows(ref, out_ref, y, base):
    flat = ref.reshape(TILES * NY, NZ)
    for at in range(0, TILES, 8):
        out_ref[base + at : base + at + 8, :] = flat[pl.ds(at * NY + y, 8, stride=NY), :]


def faces_kernel(
    direction_hbm, stiffness_hbm, low_x, high_x, low_y, high_y, direction, stiffness, sems
):
    copies = [
        pltpu.make_async_copy(direction_hbm, direction, sems.at[0]),
        pltpu.make_async_copy(stiffness_hbm, stiffness, sems.at[1]),
    ]
    for copy in copies:
        copy.start()
    for copy in copies:
        copy.wait()
    for x, out in ((0, low_x), (NX - 1, high_x)):
        out[...] = direction[:, x] * stiffness[x][None, None]
    for y, out in ((0, low_y), (NY - 1, high_y)):
        for c in range(CASES):
            for x in range(NX):
                for k in range(COMP):
                    row = (c * NX + x) * COMP + k
                    out[row : row + 1, :] = (
                        direction[c, x, k, y : y + 1, :] * stiffness[x, y : y + 1, :]
                    )


def prepare_kernel(
    residual, lower_hbm, upper_hbm, pivots_hbm, basis_hbm, prior_hbm,
    operator, solved, primal, prior_rows,
    lower, upper, pivots, basis, prior, sems,
):
    pairs = (
        (upper_hbm, upper), (lower_hbm, lower), (pivots_hbm, pivots), (basis_hbm, basis),
        (prior_hbm, prior),
    )
    copies = [
        pltpu.make_async_copy(source, target, sems.at[i])
        for i, (source, target) in enumerate(pairs)
    ]
    for copy in copies:
        copy.start()
    for copy in copies:
        copy.wait()
    for c in range(CASES):
        prior_rows[c : c + 1, :] = jnp.broadcast_to(prior[0:1, c : c + 1], (1, 128))
    both = jnp.concatenate(halves(product_of_halves(upper[...], lower[...])), axis=1)
    at = lax.broadcasted_iota(jnp.int32, (LINE, LINE), 0)
    chosen = jnp.where(at == pivots[...], 1.0, 0.0).astype(bf16)
    rows = mxu(chosen, both, NN).astype(bf16)
    rows = jnp.concatenate([rows[:, :LINE], rows[:, LINE:]], axis=0)
    picked = mxu(chosen, rows, NT).astype(bf16)
    operator[:LINE, :] = picked[:, :LINE]
    operator[LINE:, :] = picked[:, LINE:]
    local_solve(residual, operator, solved)
    primal[...] = lane_sums(restricted(basis, residual))


def by_depth_kernel(inverse, by_depth):
    for r in range(PRIMAL):
        for half in range(2):
            for part in range(3):
                at = r * 48 + half * 3 + part
                by_depth[r, half, :, part * 128 : (part + 1) * 128] = inverse[
                    pl.ds(at, 8, stride=6), :
                ]


def applied_kernel(
    direction, stiffness, coupling, below_x, above_x, below_y, above_y,
    basis, operator, solved_r, primal_r,
    applied, solved, primal, row, low_x, high_x, low_y, high_y,
):
    y_at = lax.broadcasted_iota(jnp.int32, (NY, NZ), 0)
    z_at = lax.broadcasted_iota(jnp.int32, (NY, NZ), 1)
    first_y, last_y = y_at == 0, y_at == NY - 1
    first_z, last_z = z_at == 0, z_at == NZ - 1
    curves = []
    for c in range(CASES):
        curve = None
        for x in range(NX):
            stiff = stiffness[x]
            total = direction[c, x, 0] + direction[c, x, 1] + direction[c, x, 2]
            spread = coupling[x] * total
            for k in range(COMP):
                here = direction[c, x, k]
                mine = stiff * here
                left = below_x[c, k] if x == 0 else stiffness[x - 1] * direction[c, x - 1, k]
                right = above_x[c, k] if x == NX - 1 else stiffness[x + 1] * direction[c, x + 1, k]
                at = (c * NX + x) * COMP + k
                down = jnp.where(
                    first_y,
                    jnp.broadcast_to(below_y[at : at + 1, :], (NY, NZ)),
                    pltpu.roll(mine, 1, 0),
                )
                up = jnp.where(
                    last_y,
                    jnp.broadcast_to(above_y[at : at + 1, :], (NY, NZ)),
                    pltpu.roll(mine, NY - 1, 0),
                )
                before = jnp.where(first_z, 0.0, pltpu.roll(mine, 1, 1))
                after = jnp.where(last_z, 0.0, pltpu.roll(mine, NZ - 1, 1))
                around = (left + right) + (down + up) + (before + after)
                out = stiff * (6.0 * mine - around) + spread
                applied[c, x, k] = out
                part = here * out
                curve = part if curve is None else curve + part
        curves.append(jnp.sum(curve, axis=0, keepdims=True))
    local_solve(applied, operator, solved)
    sums = restricted(basis, applied)
    whole = lane_sums(sums)
    primal[...] = whole
    stacked = jnp.concatenate([sums] + curves, axis=0)
    mine_row = lane_row(stacked)
    lane = lax.broadcasted_iota(jnp.int32, (48, 128), 1)
    sub = lax.broadcasted_iota(jnp.int32, (48, 128), 0)
    first = jnp.sum(jnp.where(lane == sub, primal_r[...], 0.0), axis=0, keepdims=True)
    row[...] = jnp.broadcast_to((first + pltpu.roll(mine_row, 48, 1))[None], (N_DEPTH, 1, 128))
    for source, base in ((solved_r, 0), (solved, CASES)):
        low_x[base : base + CASES] = source[:, 0]
        high_x[base : base + CASES] = source[:, NX - 1]
        side_rows(source, low_y, 0, base * NX * COMP)
        side_rows(source, high_y, NY - 1, base * NX * COMP)


def steps_of(table, prior):
    total = jnp.sum(table[...], axis=0, keepdims=True)
    lane = lax.broadcasted_iota(jnp.int32, (1, 128), 1)
    steps = []
    for c in range(CASES):
        curvature = jnp.sum(jnp.where(lane == 96 + c, total, 0.0), axis=1, keepdims=True)
        steps.append(prior[c : c + 1, :] / jnp.broadcast_to(curvature, (1, 128)))
    return steps


def smoothed_at(c, x, k, step, solved_r, solved_w, below_x, above_x, below_y, above_y, y_at):
    here = solved_r[c, x, k] - step * solved_w[c, x, k]
    at = (c * NX + x) * COMP + k
    under = below_y[at : at + 1, :] - step * below_y[TILES + at : TILES + at + 1, :]
    over = above_y[at : at + 1, :] - step * above_y[TILES + at : TILES + at + 1, :]
    beside = jnp.where(y_at == 0, jnp.broadcast_to(under, (NY, NZ)), 0.0)
    beside = beside + jnp.where(y_at == NY - 1, jnp.broadcast_to(over, (NY, NZ)), 0.0)
    if x == 0:
        beside = beside + (below_x[c, k] - step * below_x[CASES + c, k])
    if x == NX - 1:
        beside = beside + (above_x[c, k] - step * above_x[CASES + c, k])
    return here + 0.5 * beside


def coarse_kernel(
    prior, table, inverse, primal_r, primal_w, residual, applied, solved_r, solved_w,
    partial, steps_out, coarse, edge_x, edge_y,
):
    steps = steps_of(table, prior)
    for c in range(CASES):
        steps_out[c : c + 1, :] = steps[c]
    lane = lax.broadcasted_iota(jnp.int32, (1, 128), 1)
    weight = jnp.zeros((1, 128), f32)
    for c in range(CASES):
        weight = jnp.where(lane // PRIMAL == c, steps[c], weight)
    everything = table[...]
    primal = everything - weight * pltpu.roll(everything, 80, 1)
    high, low = halves(primal)
    pair = jnp.concatenate([high, low], axis=1)
    source = lax.broadcasted_iota(jnp.int32, (128, LINE), 0)
    target = lax.broadcasted_iota(jnp.int32, (128, LINE), 1) % PRIMAL
    slot = lax.broadcasted_iota(jnp.int32, (8, LINE), 1) // PRIMAL
    rows = []
    for c in range(CASES):
        spread = jnp.where(source == c * PRIMAL + target, 1.0, 0.0).astype(bf16)
        wide = mxu(pair, jnp.concatenate([spread, spread], axis=0), NN)
        gathered = []
        for half in range(2):
            total = None
            for group in range(16):
                for z_high in range(2):
                    at = ((half * 16 + group) * 2 + z_high) * 8
                    part = jnp.where(slot == group * 2 + z_high, wide[at : at + 8], 0.0)
                    total = part if total is None else total + part
            gathered.append(total)
        for r in range(PRIMAL):
            total = None
            for half in range(2):
                part = gathered[half] * inverse[r, half]
                total = part if total is None else total + part
            folded = total[:, 0:128] + total[:, 128:256] + total[:, 256:384]
            rows.append(jnp.sum(folded, axis=0, keepdims=True))
    coarse_values = lane_sums(jnp.concatenate(rows, axis=0))
    coarse[...] = coarse_values

    flat_r, flat_w = residual.reshape(TILES * NY, NZ), applied.reshape(TILES * NY, NZ)
    for c in range(CASES):
        step = steps[c]
        total = None
        for x in range(NX):
            for k in range(COMP):
                rest = residual[c, x, k] - step * applied[c, x, k]
                part = rest * (solved_r[c, x, k] - step * solved_w[c, x, k])
                total = part if total is None else total + part
                if x == 0 or x == NX - 1:
                    edge_x[x // (NX - 1), c, k] = 0.5 * rest
        for side, y in ((0, 0), (TILES, NY - 1)):
            for at in range(c * NX * COMP, (c + 1) * NX * COMP, 8):
                rows = pl.ds(at * NY + y, 8, stride=NY)
                edge_y[side + at : side + at + 8, :] = 0.5 * (
                    flat_r[rows, :] - step * flat_w[rows, :]
                )
        mine = slice(c * PRIMAL, (c + 1) * PRIMAL)
        own = primal_r[mine] - step * primal_w[mine]
        both = jnp.sum(own * coarse_values[mine], axis=0, keepdims=True)
        partial[c : c + 1, :] = jnp.sum(total, axis=0, keepdims=True) + jnp.where(
            lane == 0, both, 0.0
        )


def edges_kernel(
    partial, steps, edge_x, edge_y, below_x, above_x, below_y, above_y, row
):
    sums = []
    for c in range(CASES):
        step = steps[c : c + 1, :]
        total = None
        for side, halo in ((0, below_x), (1, above_x)):
            for k in range(COMP):
                part = edge_x[side, c, k] * (halo[c, k] - step * halo[CASES + c, k])
                total = part if total is None else total + part
        for side, halo in ((0, below_y), (TILES, above_y)):
            for at in range(c * NX * COMP, (c + 1) * NX * COMP, 8):
                beside = halo[at : at + 8, :] - step * halo[TILES + at : TILES + at + 8, :]
                total = total + edge_y[side + at : side + at + 8, :] * beside
        sums.append(jnp.sum(total, axis=0, keepdims=True))
    whole = jnp.concatenate(sums, axis=0) + partial[...]
    row[...] = jnp.broadcast_to(lane_row(whole)[None], (N_DEPTH, 1, 128))


def spread_kernel(line, out):
    out[...] = jnp.broadcast_to(line[...][None], (N_PLANE, N_DEPTH, 128))


def fold_kernel(line, out):
    total = jnp.sum(line[...], axis=0, keepdims=True)
    out[...] = jnp.broadcast_to(total, (N_PLANE, 1, 128))


def advance_kernel(
    steps, solution, residual, direction, applied, solution_next, residual_next
):
    for c in range(CASES):
        step = steps[c : c + 1, :]
        for x in range(NX):
            for k in range(COMP):
                residual_next[c, x, k] = residual[c, x, k] - step * applied[c, x, k]
                solution_next[c, x, k] = solution[c, x, k] + step * direction[c, x, k]


def precondition_kernel(
    steps, coarse, basis, direction, solved_r, solved_w, below_x, above_x, below_y, above_y,
    preconditioned, held,
):
    held[...] = direction[...]
    y_at = lax.broadcasted_iota(jnp.int32, (NY, NZ), 0)
    for c in range(CASES):
        step = steps[c : c + 1, :]
        for x in range(NX):
            for k in range(COMP):
                out = smoothed_at(
                    c, x, k, step, solved_r, solved_w, below_x, above_x, below_y, above_y, y_at
                )
                for p in range(NP):
                    at = c * PRIMAL + k * NP + p
                    out = out + basis[p, x] * coarse[at : at + 1, :]
                preconditioned[c, x, k] = out


def final_kernel(prior, parts, preconditioned, direction, direction_next, inner):
    total = jnp.sum(parts[...], axis=0, keepdims=True)
    inner[...] = total[0, :CASES]
    lane = lax.broadcasted_iota(jnp.int32, (1, 128), 1)
    for c in range(CASES):
        mine = jnp.sum(jnp.where(lane == c, total, 0.0), axis=1, keepdims=True)
        growth = jnp.broadcast_to(mine, (1, NZ)) / prior[c : c + 1, :]
        for x in range(NX):
            for k in range(COMP):
                direction_next[c, x, k] = (
                    preconditioned[c, x, k] + growth * direction[c, x, k]
                )


VMEM = pl.BlockSpec(memory_space=pltpu.VMEM)
HBM = pl.BlockSpec(memory_space=pltpu.HBM)


def local_call(body, outs, spaces, *args, scratch=()):
    specs = [{"v": VMEM, "h": HBM}[space] for space in spaces]
    specs += [VMEM] * (len(args) - len(specs))
    args = tuple(
        pltpu.with_memory_space_constraint(arg, pltpu.HBM) if spec is HBM else arg
        for arg, spec in zip(args, specs)
    )
    return pl.pallas_call(
        body,
        out_shape=[
            shape if hasattr(shape, "dtype") else jax.ShapeDtypeStruct(shape, f32)
            for shape in outs
        ],
        in_specs=specs,
        out_specs=[VMEM] * len(outs),
        scratch_shapes=list(scratch),
        compiler_params=pltpu.CompilerParams(vmem_limit_bytes=20 << 20),
    )(*args)


def exchange(rows, axes):
    return lax.all_to_all(rows, axes, 0, 0, tiled=True)


def neighbours(low, high, axes, count):
    up = [(i, i + 1) for i in range(count - 1)]
    down = [(i + 1, i) for i in range(count - 1)]
    return lax.ppermute(high, axes, up), lax.ppermute(low, axes, down)


def body(
    solution, residual, direction, stiffness, coupling, lower_factor, upper_factor,
    pivot_order, coarse_basis, coarse_inverse, inner_prior,
):
    solution, residual, direction = (
        a.transpose(0, 1, 3, 2, 4) for a in (solution, residual, direction)
    )
    end_x = (CASES, COMP, NY, NZ)
    end_y = (TILES, NZ)
    low_x, high_x, low_y, high_y = local_call(
        faces_kernel, [end_x, end_x, end_y, end_y], "hh", direction, stiffness,
        scratch=[
            pltpu.VMEM(FIELD, f32), pltpu.VMEM((NX, NY, NZ), f32), pltpu.SemaphoreType.DMA((2,)),
        ],
    )
    below_y, above_y = neighbours(low_y, high_y, YZ_AXES, N_YZ)
    below_x, above_x = neighbours(low_x, high_x, GX_AXES, N_GX)

    operator, solved_r, primal_r, prior_rows = local_call(
        prepare_kernel, [OPERATOR, FIELD, (48, 128), (CASES, 128)], "vhhhhh",
        residual, lower_factor[0, 0], upper_factor[0, 0], pivot_order[0], coarse_basis,
        inner_prior.reshape(1, CASES),
        scratch=[
            pltpu.VMEM((LINE, LINE), f32), pltpu.VMEM((LINE, LINE), f32),
            pltpu.VMEM((1, LINE), jnp.int32), pltpu.VMEM((NP, NX, NY, NZ), f32),
            pltpu.VMEM((1, CASES), f32), pltpu.SemaphoreType.DMA((5,)),
        ],
    )

    twice_x = (2 * CASES, COMP, NY, NZ)
    twice_y = (2 * TILES, NZ)
    rows_z = (N_DEPTH, 1, 128)
    applied, solved_w, primal_w, rows, low_x, high_x, low_y, high_y = local_call(
        applied_kernel,
        [FIELD, FIELD, (48, 128), rows_z, twice_x, twice_x, twice_y, twice_y], "",
        direction, stiffness, coupling, below_x, above_x, below_y, above_y,
        coarse_basis, operator, solved_r, primal_r,
    )

    line = exchange(rows, DEPTH)
    below_y, above_y = neighbours(low_y, high_y, YZ_AXES, N_YZ)
    below_x, above_x = neighbours(low_x, high_x, GX_AXES, N_GX)
    (inverse,) = local_call(
        by_depth_kernel, [(PRIMAL, 2, 8, LINE)], "",
        coarse_inverse.reshape(PRIMAL * 48, 128),
    )
    (lines,) = local_call(spread_kernel, [(N_PLANE, N_DEPTH, 128)], "", line.reshape(N_DEPTH, 128))
    table = exchange(lines, PLANE)
    table = table.reshape(N_PLANE * N_DEPTH, 128)

    halo = (below_x, above_x, below_y, above_y)
    partial, steps, coarse, edge_x, edge_y = local_call(
        coarse_kernel,
        [(CASES, 128), (CASES, 128), (48, 128), (2, CASES, COMP, NY, NZ), (2 * TILES, NZ)], "",
        prior_rows, table, inverse, primal_r, primal_w, residual, applied, solved_r, solved_w,
    )
    (rows,) = local_call(edges_kernel, [rows_z], "", partial, steps, edge_x, edge_y, *halo)
    line = exchange(rows, DEPTH)
    solution_next, residual_next = local_call(
        advance_kernel, [FIELD, FIELD], "",
        steps, solution, residual, direction, applied,
    )
    (rows,) = local_call(fold_kernel, [(N_PLANE, 1, 128)], "", line)
    parts = exchange(rows, PLANE)
    preconditioned, held = local_call(
        precondition_kernel, [FIELD, FIELD], "",
        steps, coarse, coarse_basis, direction, solved_r, solved_w, *halo,
    )
    direction_next, inner = local_call(
        final_kernel, [FIELD, (CASES,)], "",
        prior_rows, parts.reshape(N_PLANE, 128), preconditioned, held,
    )
    solution_next, residual_next, direction_next = (
        a.transpose(0, 1, 3, 2, 4) for a in (solution_next, residual_next, direction_next)
    )
    return (solution_next, residual_next, direction_next, inner)


def solution(mesh):
    fine = Mesh(mesh.devices.reshape(8, 4, 2, 4, 2), ("zl", "x", "c", "y", "zh"))
    field = P(None, GX_AXES, YZ_AXES, None, None)
    block = P(GX_AXES, YZ_AXES, None)
    factor = P(GX_AXES, YZ_AXES, None, None)
    in_specs = (
        field, field, field, block, block, factor, factor, block,
        P(None, GX_AXES, YZ_AXES, None), factor, P(),
    )
    return jax.shard_map(
        body,
        mesh=fine,
        in_specs=in_specs,
        out_specs=(field, field, field, P()),
        check_vma=False,
    )
```

```python
import jax
import jax.numpy as jnp
from jax import lax
from jax.experimental import pallas as pl
from jax.experimental.pallas import tpu as pltpu
from jax.sharding import Mesh, PartitionSpec as P


DEPTH = ("zh", "zl")
PLANE = ("x", "c", "y")
GX_AXES = ("zl", "x", "c")
YZ_AXES = ("y", "zh")
N_DEPTH = 16
N_PLANE = 32
N_GX = 64
N_YZ = 8

CASES, NX, COMP, NY, NZ = 4, 8, 3, 8, 128
NP = 4
PRIMAL = COMP * NP
LINE = COMP * NZ
TILES = CASES * NX * COMP
FIELD = (CASES, NX, COMP, NY, NZ)
f32 = jnp.float32
bf16 = jnp.bfloat16
OPERATOR = jax.ShapeDtypeStruct((2 * LINE, LINE), bf16)
NT = (((1,), (1,)), ((), ()))
NN = (((1,), (0,)), ((), ()))


def mxu(a, b, dims):
    return lax.dot_general(a, b, dims, preferred_element_type=f32)


def halves(a):
    high = a.astype(bf16)
    return high, (a - high.astype(f32)).astype(bf16)


def thirds(a):
    high = a.astype(bf16)
    rest = a - high.astype(f32)
    mid = rest.astype(bf16)
    return high, mid, (rest - mid.astype(f32)).astype(bf16)


def product_of_halves(a, b):
    a0, a1 = halves(a)
    b0, b1 = halves(b)
    return mxu(
        jnp.concatenate([a0, a0, a1], axis=1), jnp.concatenate([b0, b1, b0], axis=0), NN
    )


def lane_sums(a):
    ones = jnp.ones((a.shape[1], 128), bf16)
    a0, a1, a2 = thirds(a)
    return (mxu(a2, ones, NN) + mxu(a1, ones, NN)) + mxu(a0, ones, NN)


def lane_row(a):
    rows = a.shape[0]
    if rows < 128:
        a = jnp.concatenate([a, jnp.zeros((128 - rows, 128), f32)], axis=0)
    ones = jnp.ones((8, 128), bf16)
    a0, a1, a2 = thirds(a)
    return ((mxu(ones, a2, NT) + mxu(ones, a1, NT)) + mxu(ones, a0, NT))[0:1]


def restricted(basis, field):
    rows = []
    for c in range(CASES):
        for k in range(COMP):
            for p in range(NP):
                total = basis[p, 0] * field[c, 0, k]
                for x in range(1, NX):
                    total = total + basis[p, x] * field[c, x, k]
                rows.append(jnp.sum(total, axis=0, keepdims=True))
    return jnp.concatenate(rows, axis=0)


def local_solve(field, operator, out_ref):
    rows = [field[:, :, k].reshape(CASES * NX * NY, NZ) for k in range(COMP)]
    parts = [thirds(row) for row in rows]
    high, mid, low = (jnp.concatenate([part[i] for part in parts], axis=1) for i in range(3))
    whole = operator[...]
    first, second = whole[:LINE], whole[LINE:]
    total = mxu(
        jnp.concatenate([low, mid, high, mid, high], axis=1),
        jnp.concatenate([first, second, second, first, first], axis=0),
        NN,
    )
    for k in range(COMP):
        out_ref[:, :, k] = total[:, k * NZ : (k + 1) * NZ].reshape(CASES, NX, NY, NZ)


def side_rows(ref, out_ref, y, base):
    flat = ref.reshape(TILES * NY, NZ)
    for at in range(0, TILES, 8):
        out_ref[base + at : base + at + 8, :] = flat[pl.ds(at * NY + y, 8, stride=NY), :]


def faces_kernel(
    direction_hbm, stiffness_hbm, low_x, high_x, low_y, high_y, direction, stiffness, sems
):
    copies = [
        pltpu.make_async_copy(direction_hbm, direction, sems.at[0]),
        pltpu.make_async_copy(stiffness_hbm, stiffness, sems.at[1]),
    ]
    for copy in copies:
        copy.start()
    for copy in copies:
        copy.wait()
    for x, out in ((0, low_x), (NX - 1, high_x)):
        out[...] = direction[:, x] * stiffness[x][None, None]
    for y, out in ((0, low_y), (NY - 1, high_y)):
        for c in range(CASES):
            for x in range(NX):
                for k in range(COMP):
                    row = (c * NX + x) * COMP + k
                    out[row : row + 1, :] = (
                        direction[c, x, k, y : y + 1, :] * stiffness[x, y : y + 1, :]
                    )


def prepare_kernel(
    residual, lower_hbm, upper_hbm, pivots_hbm, basis_hbm, prior_hbm,
    operator, solved, primal, prior_rows,
    lower, upper, pivots, basis, prior, sems,
):
    pairs = (
        (upper_hbm, upper), (lower_hbm, lower), (pivots_hbm, pivots), (basis_hbm, basis),
        (prior_hbm, prior),
    )
    copies = [
        pltpu.make_async_copy(source, target, sems.at[i])
        for i, (source, target) in enumerate(pairs)
    ]
    for copy in copies:
        copy.start()
    for copy in copies:
        copy.wait()
    for c in range(CASES):
        prior_rows[c : c + 1, :] = jnp.broadcast_to(prior[0:1, c : c + 1], (1, 128))
    both = jnp.concatenate(halves(product_of_halves(upper[...], lower[...])), axis=1)
    at = lax.broadcasted_iota(jnp.int32, (LINE, LINE), 0)
    chosen = jnp.where(at == pivots[...], 1.0, 0.0).astype(bf16)
    rows = mxu(chosen, both, NN).astype(bf16)
    rows = jnp.concatenate([rows[:, :LINE], rows[:, LINE:]], axis=0)
    picked = mxu(chosen, rows, NT).astype(bf16)
    operator[:LINE, :] = picked[:, :LINE]
    operator[LINE:, :] = picked[:, LINE:]
    local_solve(residual, operator, solved)
    primal[...] = lane_sums(restricted(basis, residual))


def by_depth_kernel(inverse, by_depth):
    for r in range(PRIMAL):
        for half in range(2):
            for part in range(3):
                at = r * 48 + half * 3 + part
                by_depth[r, half, :, part * 128 : (part + 1) * 128] = inverse[
                    pl.ds(at, 8, stride=6), :
                ]


def applied_kernel(
    direction, stiffness, coupling, below_x, above_x, below_y, above_y,
    basis, operator, solved_r, primal_r,
    applied, solved, primal, row, low_x, high_x, low_y, high_y,
):
    y_at = lax.broadcasted_iota(jnp.int32, (NY, NZ), 0)
    z_at = lax.broadcasted_iota(jnp.int32, (NY, NZ), 1)
    first_y, last_y = y_at == 0, y_at == NY - 1
    first_z, last_z = z_at == 0, z_at == NZ - 1
    curves = []
    for c in range(CASES):
        curve = None
        for x in range(NX):
            stiff = stiffness[x]
            total = direction[c, x, 0] + direction[c, x, 1] + direction[c, x, 2]
            spread = coupling[x] * total
            for k in range(COMP):
                here = direction[c, x, k]
                mine = stiff * here
                left = below_x[c, k] if x == 0 else stiffness[x - 1] * direction[c, x - 1, k]
                right = above_x[c, k] if x == NX - 1 else stiffness[x + 1] * direction[c, x + 1, k]
                at = (c * NX + x) * COMP + k
                down = jnp.where(
                    first_y,
                    jnp.broadcast_to(below_y[at : at + 1, :], (NY, NZ)),
                    pltpu.roll(mine, 1, 0),
                )
                up = jnp.where(
                    last_y,
                    jnp.broadcast_to(above_y[at : at + 1, :], (NY, NZ)),
                    pltpu.roll(mine, NY - 1, 0),
                )
                before = jnp.where(first_z, 0.0, pltpu.roll(mine, 1, 1))
                after = jnp.where(last_z, 0.0, pltpu.roll(mine, NZ - 1, 1))
                around = (left + right) + (down + up) + (before + after)
                out = stiff * (6.0 * mine - around) + spread
                applied[c, x, k] = out
                part = here * out
                curve = part if curve is None else curve + part
        curves.append(jnp.sum(curve, axis=0, keepdims=True))
    local_solve(applied, operator, solved)
    sums = restricted(basis, applied)
    whole = lane_sums(sums)
    primal[...] = whole
    stacked = jnp.concatenate([sums] + curves, axis=0)
    mine_row = lane_row(stacked)
    lane = lax.broadcasted_iota(jnp.int32, (48, 128), 1)
    sub = lax.broadcasted_iota(jnp.int32, (48, 128), 0)
    first = jnp.sum(jnp.where(lane == sub, primal_r[...], 0.0), axis=0, keepdims=True)
    row[...] = jnp.broadcast_to((first + pltpu.roll(mine_row, 48, 1))[None], (N_DEPTH, 1, 128))
    for source, base in ((solved_r, 0), (solved, CASES)):
        low_x[base : base + CASES] = source[:, 0]
        high_x[base : base + CASES] = source[:, NX - 1]
        side_rows(source, low_y, 0, base * NX * COMP)
        side_rows(source, high_y, NY - 1, base * NX * COMP)


def steps_of(table, prior):
    total = jnp.sum(table[...], axis=0, keepdims=True)
    lane = lax.broadcasted_iota(jnp.int32, (1, 128), 1)
    steps = []
    for c in range(CASES):
        curvature = jnp.sum(jnp.where(lane == 96 + c, total, 0.0), axis=1, keepdims=True)
        steps.append(prior[c : c + 1, :] / jnp.broadcast_to(curvature, (1, 128)))
    return steps


def smoothed_at(c, x, k, step, solved_r, solved_w, below_x, above_x, below_y, above_y, y_at):
    here = solved_r[c, x, k] - step * solved_w[c, x, k]
    at = (c * NX + x) * COMP + k
    under = below_y[at : at + 1, :] - step * below_y[TILES + at : TILES + at + 1, :]
    over = above_y[at : at + 1, :] - step * above_y[TILES + at : TILES + at + 1, :]
    beside = jnp.where(y_at == 0, jnp.broadcast_to(under, (NY, NZ)), 0.0)
    beside = beside + jnp.where(y_at == NY - 1, jnp.broadcast_to(over, (NY, NZ)), 0.0)
    if x == 0:
        beside = beside + (below_x[c, k] - step * below_x[CASES + c, k])
    if x == NX - 1:
        beside = beside + (above_x[c, k] - step * above_x[CASES + c, k])
    return here + 0.5 * beside


def coarse_kernel(
    prior, table, inverse, primal_r, primal_w, residual, applied, solved_r, solved_w,
    partial, steps_out, coarse, edge_x, edge_y,
):
    steps = steps_of(table, prior)
    for c in range(CASES):
        steps_out[c : c + 1, :] = steps[c]
    lane = lax.broadcasted_iota(jnp.int32, (1, 128), 1)
    weight = jnp.zeros((1, 128), f32)
    for c in range(CASES):
        weight = jnp.where(lane // PRIMAL == c, steps[c], weight)
    everything = table[...]
    primal = everything - weight * pltpu.roll(everything, 80, 1)
    high, low = halves(primal)
    pair = jnp.concatenate([high, low], axis=1)
    source = lax.broadcasted_iota(jnp.int32, (128, LINE), 0)
    target = lax.broadcasted_iota(jnp.int32, (128, LINE), 1) % PRIMAL
    slot = lax.broadcasted_iota(jnp.int32, (8, LINE), 1) // PRIMAL
    rows = []
    for c in range(CASES):
        spread = jnp.where(source == c * PRIMAL + target, 1.0, 0.0).astype(bf16)
        wide = mxu(pair, jnp.concatenate([spread, spread], axis=0), NN)
        gathered = []
        for half in range(2):
            total = None
            for group in range(16):
                for z_high in range(2):
                    at = ((half * 16 + group) * 2 + z_high) * 8
                    part = jnp.where(slot == group * 2 + z_high, wide[at : at + 8], 0.0)
                    total = part if total is None else total + part
            gathered.append(total)
        for r in range(PRIMAL):
            total = None
            for half in range(2):
                part = gathered[half] * inverse[r, half]
                total = part if total is None else total + part
            folded = total[:, 0:128] + total[:, 128:256] + total[:, 256:384]
            rows.append(jnp.sum(folded, axis=0, keepdims=True))
    coarse_values = lane_sums(jnp.concatenate(rows, axis=0))
    coarse[...] = coarse_values

    flat_r, flat_w = residual.reshape(TILES * NY, NZ), applied.reshape(TILES * NY, NZ)
    for c in range(CASES):
        step = steps[c]
        total = None
        for x in range(NX):
            for k in range(COMP):
                rest = residual[c, x, k] - step * applied[c, x, k]
                part = rest * (solved_r[c, x, k] - step * solved_w[c, x, k])
                total = part if total is None else total + part
                if x == 0 or x == NX - 1:
                    edge_x[x // (NX - 1), c, k] = 0.5 * rest
        for side, y in ((0, 0), (TILES, NY - 1)):
            for at in range(c * NX * COMP, (c + 1) * NX * COMP, 8):
                rows = pl.ds(at * NY + y, 8, stride=NY)
                edge_y[side + at : side + at + 8, :] = 0.5 * (
                    flat_r[rows, :] - step * flat_w[rows, :]
                )
        mine = slice(c * PRIMAL, (c + 1) * PRIMAL)
        own = primal_r[mine] - step * primal_w[mine]
        both = jnp.sum(own * coarse_values[mine], axis=0, keepdims=True)
        partial[c : c + 1, :] = jnp.sum(total, axis=0, keepdims=True) + jnp.where(
            lane == 0, both, 0.0
        )


def edges_kernel(
    partial, steps, edge_x, edge_y, below_x, above_x, below_y, above_y, row
):
    sums = []
    for c in range(CASES):
        step = steps[c : c + 1, :]
        total = None
        for side, halo in ((0, below_x), (1, above_x)):
            for k in range(COMP):
                part = edge_x[side, c, k] * (halo[c, k] - step * halo[CASES + c, k])
                total = part if total is None else total + part
        for side, halo in ((0, below_y), (TILES, above_y)):
            for at in range(c * NX * COMP, (c + 1) * NX * COMP, 8):
                beside = halo[at : at + 8, :] - step * halo[TILES + at : TILES + at + 8, :]
                total = total + edge_y[side + at : side + at + 8, :] * beside
        sums.append(jnp.sum(total, axis=0, keepdims=True))
    whole = jnp.concatenate(sums, axis=0) + partial[...]
    row[...] = jnp.broadcast_to(lane_row(whole)[None], (N_DEPTH, 1, 128))


def spread_kernel(line, out):
    out[...] = jnp.broadcast_to(line[...][None], (N_PLANE, N_DEPTH, 128))


def fold_kernel(line, out):
    total = jnp.sum(line[...], axis=0, keepdims=True)
    out[...] = jnp.broadcast_to(total, (N_PLANE, 1, 128))


def advance_kernel(
    steps, solution, residual, direction, applied, solution_next, residual_next
):
    for c in range(CASES):
        step = steps[c : c + 1, :]
        for x in range(NX):
            for k in range(COMP):
                residual_next[c, x, k] = residual[c, x, k] - step * applied[c, x, k]
                solution_next[c, x, k] = solution[c, x, k] + step * direction[c, x, k]


def precondition_kernel(
    steps, coarse, basis, solved_r, solved_w, below_x, above_x, below_y, above_y, preconditioned
):
    y_at = lax.broadcasted_iota(jnp.int32, (NY, NZ), 0)
    for c in range(CASES):
        step = steps[c : c + 1, :]
        for x in range(NX):
            for k in range(COMP):
                out = smoothed_at(
                    c, x, k, step, solved_r, solved_w, below_x, above_x, below_y, above_y, y_at
                )
                for p in range(NP):
                    at = c * PRIMAL + k * NP + p
                    out = out + basis[p, x] * coarse[at : at + 1, :]
                preconditioned[c, x, k] = out


def final_kernel(
    prior, parts, preconditioned_hbm, direction_hbm, direction_next_hbm, inner,
    preconditioned, direction, direction_next, in_sems, out_sems,
):
    copies_in, copies_out = [], []
    for c in range(CASES):
        copies_in.append(
            (
                pltpu.make_async_copy(
                    preconditioned_hbm.at[c], preconditioned.at[c], in_sems.at[0, c]
                ),
                pltpu.make_async_copy(direction_hbm.at[c], direction.at[c], in_sems.at[1, c]),
            )
        )
        copies_out.append(
            pltpu.make_async_copy(direction_next.at[c], direction_next_hbm.at[c], out_sems.at[c])
        )
        for copy in copies_in[c]:
            copy.start()
    total = jnp.sum(parts[...], axis=0, keepdims=True)
    inner[...] = total[0, :CASES]
    lane = lax.broadcasted_iota(jnp.int32, (1, 128), 1)
    growth = []
    for c in range(CASES):
        mine = jnp.sum(jnp.where(lane == c, total, 0.0), axis=1, keepdims=True)
        growth.append(jnp.broadcast_to(mine, (1, NZ)) / prior[c : c + 1, :])
    for c in range(CASES):
        for copy in copies_in[c]:
            copy.wait()
        for x in range(NX):
            for k in range(COMP):
                direction_next[c, x, k] = (
                    preconditioned[c, x, k] + growth[c] * direction[c, x, k]
                )
        copies_out[c].start()
    for copy in copies_out:
        copy.wait()


VMEM = pl.BlockSpec(memory_space=pltpu.VMEM)
HBM = pl.BlockSpec(memory_space=pltpu.HBM)


def local_call(body, outs, spaces, *args, scratch=(), results=""):
    specs = [{"v": VMEM, "h": HBM}[space] for space in spaces]
    specs += [VMEM] * (len(args) - len(specs))
    args = tuple(
        pltpu.with_memory_space_constraint(arg, pltpu.HBM) if spec is HBM else arg
        for arg, spec in zip(args, specs)
    )
    return pl.pallas_call(
        body,
        out_shape=[
            shape if hasattr(shape, "dtype") else jax.ShapeDtypeStruct(shape, f32)
            for shape in outs
        ],
        in_specs=specs,
        out_specs=[HBM if space == "h" else VMEM for space in results.ljust(len(outs), "v")],
        scratch_shapes=list(scratch),
        compiler_params=pltpu.CompilerParams(vmem_limit_bytes=20 << 20),
    )(*args)


def exchange(rows, axes):
    return lax.all_to_all(rows, axes, 0, 0, tiled=True)


def neighbours(low, high, axes, count):
    up = [(i, i + 1) for i in range(count - 1)]
    down = [(i + 1, i) for i in range(count - 1)]
    return lax.ppermute(high, axes, up), lax.ppermute(low, axes, down)


def body(
    solution, residual, direction, stiffness, coupling, lower_factor, upper_factor,
    pivot_order, coarse_basis, coarse_inverse, inner_prior,
):
    solution, residual, direction = (
        a.transpose(0, 1, 3, 2, 4) for a in (solution, residual, direction)
    )
    end_x = (CASES, COMP, NY, NZ)
    end_y = (TILES, NZ)
    low_x, high_x, low_y, high_y = local_call(
        faces_kernel, [end_x, end_x, end_y, end_y], "hh", direction, stiffness,
        scratch=[
            pltpu.VMEM(FIELD, f32), pltpu.VMEM((NX, NY, NZ), f32), pltpu.SemaphoreType.DMA((2,)),
        ],
    )
    below_y, above_y = neighbours(low_y, high_y, YZ_AXES, N_YZ)
    below_x, above_x = neighbours(low_x, high_x, GX_AXES, N_GX)

    operator, solved_r, primal_r, prior_rows = local_call(
        prepare_kernel, [OPERATOR, FIELD, (48, 128), (CASES, 128)], "vhhhhh",
        residual, lower_factor[0, 0], upper_factor[0, 0], pivot_order[0], coarse_basis,
        inner_prior.reshape(1, CASES),
        scratch=[
            pltpu.VMEM((LINE, LINE), f32), pltpu.VMEM((LINE, LINE), f32),
            pltpu.VMEM((1, LINE), jnp.int32), pltpu.VMEM((NP, NX, NY, NZ), f32),
            pltpu.VMEM((1, CASES), f32), pltpu.SemaphoreType.DMA((5,)),
        ],
    )

    twice_x = (2 * CASES, COMP, NY, NZ)
    twice_y = (2 * TILES, NZ)
    rows_z = (N_DEPTH, 1, 128)
    applied, solved_w, primal_w, rows, low_x, high_x, low_y, high_y = local_call(
        applied_kernel,
        [FIELD, FIELD, (48, 128), rows_z, twice_x, twice_x, twice_y, twice_y], "",
        direction, stiffness, coupling, below_x, above_x, below_y, above_y,
        coarse_basis, operator, solved_r, primal_r,
    )

    line = exchange(rows, DEPTH)
    below_y, above_y = neighbours(low_y, high_y, YZ_AXES, N_YZ)
    below_x, above_x = neighbours(low_x, high_x, GX_AXES, N_GX)
    (inverse,) = local_call(
        by_depth_kernel, [(PRIMAL, 2, 8, LINE)], "",
        coarse_inverse.reshape(PRIMAL * 48, 128),
    )
    (lines,) = local_call(spread_kernel, [(N_PLANE, N_DEPTH, 128)], "", line.reshape(N_DEPTH, 128))
    table = exchange(lines, PLANE)
    table = table.reshape(N_PLANE * N_DEPTH, 128)

    halo = (below_x, above_x, below_y, above_y)
    partial, steps, coarse, edge_x, edge_y = local_call(
        coarse_kernel,
        [(CASES, 128), (CASES, 128), (48, 128), (2, CASES, COMP, NY, NZ), (2 * TILES, NZ)], "",
        prior_rows, table, inverse, primal_r, primal_w, residual, applied, solved_r, solved_w,
    )
    (rows,) = local_call(edges_kernel, [rows_z], "", partial, steps, edge_x, edge_y, *halo)
    line = exchange(rows, DEPTH)
    solution_next, residual_next = local_call(
        advance_kernel, [FIELD, FIELD], "",
        steps, solution, residual, direction, applied,
    )
    (rows,) = local_call(fold_kernel, [(N_PLANE, 1, 128)], "", line)
    parts = exchange(rows, PLANE)
    (preconditioned,) = local_call(
        precondition_kernel, [FIELD], "",
        steps, coarse, coarse_basis, solved_r, solved_w, *halo,
    )
    direction_next, inner = local_call(
        final_kernel, [FIELD, (CASES,)], "vvhh",
        prior_rows, parts.reshape(N_PLANE, 128), preconditioned, direction,
        scratch=[pltpu.VMEM(FIELD, f32)] * 3
        + [pltpu.SemaphoreType.DMA((2, CASES)), pltpu.SemaphoreType.DMA((CASES,))],
        results="hv",
    )
    solution_next, residual_next, direction_next = (
        a.transpose(0, 1, 3, 2, 4) for a in (solution_next, residual_next, direction_next)
    )
    return (solution_next, residual_next, direction_next, inner)


def solution(mesh):
    fine = Mesh(mesh.devices.reshape(8, 4, 2, 4, 2), ("zl", "x", "c", "y", "zh"))
    field = P(None, GX_AXES, YZ_AXES, None, None)
    block = P(GX_AXES, YZ_AXES, None)
    factor = P(GX_AXES, YZ_AXES, None, None)
    in_specs = (
        field, field, field, block, block, factor, factor, block,
        P(None, GX_AXES, YZ_AXES, None), factor, P(),
    )
    return jax.shard_map(
        body,
        mesh=fine,
        in_specs=in_specs,
        out_specs=(field, field, field, P()),
        check_vma=False,
    )
```
